128 devices in a mesh: row: 8 (over x, core), col: 16 (over y, z).
Axes of the slice: x: 4, y: 4, z: 4, core: 2. Of those that a mesh axis runs over, the one named last changes fastest.
Arguments:
- valence: bfloat16 [2, 16, 32768], replicated, may hold values from -6 to 6
- conduction: bfloat16 [2, 128, 32768], replicated, may hold values from -6 to 6
- valence_energy: float32 [16], replicated, may hold values from -8 to -1
- conduction_energy: float32 [128], replicated, may hold values from 0.5 to 6
- band_pairs: int32 [1024, 2], P(('row', 'col')), may hold values from 0 to 127, as said below
- grid_index: int32 [16384], replicated, may hold values from 0 to 32767, as said below
Outputs:
- response: float32 [2, 16384, 16384], P(None, 'row', 'col')
The draws below stay inside these ranges and needn't reach their ends.
Inputs may be any that keep to these rules, and one draw needn't show every extreme that they name: `band_pairs`: the rows are distinct combinations of a valence band below 16 and a conduction band below 128, half of all combinations. `grid_index`: the 16384 entries are distinct.
All inputs are finite; a program needn't handle non-finite values.
Results may differ from the reference program's by a relative error of at most 0.0039.
Values may be sent and summed in bfloat16 or wider, within the bound.
A program may use at most 192 MiB of HBM per device.

```python
import math
import jax
import jax.numpy as jnp
from jax import lax

NG = 16384
N1 = 32
N2 = 32
N3 = 32
NVB = 16
NCB = 128
NR = 32768


def draw_band_pairs(key, part):
    combos = NVB * NCB
    target = NCB - 1
    others = jax.random.permutation(key, combos - 1).astype(jnp.int32)
    others = jnp.where(others >= target, others + 1, others)
    chosen = jnp.concatenate([jnp.array([target], dtype=jnp.int32), others[:NVB * NCB // 2 - 1]])
    chosen = jax.random.permutation(jax.random.fold_in(key, 5), chosen).astype(jnp.int32)
    return jnp.stack([chosen // NCB, chosen % NCB], axis=1).astype(jnp.int32)


def draw_grid_index(key, part):
    inner = 1 + jax.random.permutation(jax.random.fold_in(key, 11), NR - 2)[:NG - 2]
    ends = jnp.array([0, NR - 1], dtype=jnp.int32)
    joined = jnp.concatenate([ends, inner.astype(jnp.int32)])
    shuffled = jax.random.permutation(jax.random.fold_in(key, 23), joined)
    return shuffled.astype(jnp.int32)


def gaussian(stream_key, dims, spread, limit, kind=jnp.bfloat16):
    return jnp.clip(spread * jax.random.normal(stream_key, dims, jnp.float32), -limit, limit).astype(kind)


def setup_inputs(seed: int = 0) -> dict:
    seeds = jax.random.split(jax.random.key(seed), 7)
    return {
        "valence": gaussian(seeds[0], (2, NVB, NR), 0.7071, 6.0),
        "conduction": gaussian(seeds[1], (2, NCB, NR), 0.7071, 6.0),
        "valence_energy": jnp.clip(jax.random.uniform(seeds[2], (NVB,), jnp.float32, -8.0, -1.0), -8.0, -1.0),
        "conduction_energy": jnp.clip(jax.random.uniform(seeds[3], (NCB,), jnp.float32, 0.5, 6.0), 0.5, 6.0),
        "band_pairs": draw_band_pairs(jax.random.fold_in(seeds[6], 71), 0),
        "grid_index": draw_grid_index(jax.random.fold_in(seeds[6], 71), 0),
    }


def tables(length):
    position = jnp.arange(length, dtype=jnp.int32)
    phase_angle = (position[:, None] * position[None, :] % length).astype(jnp.float32) * (2.0 * math.pi / length)
    return (jnp.cos(phase_angle), jnp.sin(phase_angle))

def transform(real_part, imag_part):
    for pattern, length in (('pabr,kr->pabk', N3), ('parc,kr->pakc', N2), ('prbc,kr->pkbc', N1)):
        cosine, sine_table = tables(length)
        new_real = jnp.einsum(pattern, real_part, cosine, precision=lax.Precision.HIGHEST) + jnp.einsum(pattern, imag_part, sine_table, precision=lax.Precision.HIGHEST)
        new_imag = jnp.einsum(pattern, imag_part, cosine, precision=lax.Precision.HIGHEST) - jnp.einsum(pattern, real_part, sine_table, precision=lax.Precision.HIGHEST)
        real_part, imag_part = (new_real, new_imag)
    return (real_part, imag_part)

def pair_spectrum(valence, conduction, valence_energy, conduction_energy, band_pairs):
    pair_count = band_pairs.shape[0]
    valence_rows = jnp.take(valence, band_pairs[:, 0], axis=1).astype(jnp.float32)
    conduction_rows = jnp.take(conduction, band_pairs[:, 1], axis=1).astype(jnp.float32)
    rho_real = valence_rows[0] * conduction_rows[0] + valence_rows[1] * conduction_rows[1]
    rho_imag = valence_rows[0] * conduction_rows[1] - valence_rows[1] * conduction_rows[0]
    grid_shape = (pair_count, N1, N2, N3)
    out_real, out_imag = transform(rho_real.reshape(grid_shape), rho_imag.reshape(grid_shape))
    normalize = 1.0 / math.sqrt(N1 * N2 * N3)
    spectrum = jnp.stack([out_real.reshape(pair_count, -1), out_imag.reshape(pair_count, -1)]) * normalize
    valence_hot = band_pairs[:, 0][:, None] == jnp.arange(valence_energy.shape[0], dtype=jnp.int32)[None, :]
    conduction_hot = band_pairs[:, 1][:, None] == jnp.arange(conduction_energy.shape[0], dtype=jnp.int32)[None, :]
    energy_gap = lax.optimization_barrier(jnp.sum(jnp.where(valence_hot, valence_energy[None, :], 0.0), axis=1)) - lax.optimization_barrier(jnp.sum(jnp.where(conduction_hot, conduction_energy[None, :], 0.0), axis=1))
    weights = 2.0 / (math.sqrt(NVB * NCB // 2) * energy_gap)
    return (spectrum, weights)

def contract(weighted_part, operand, crossed):
    contract_dims = (((0, 1), (0, 1)), ((), ()))
    real_part = lax.dot_general(weighted_part, operand, contract_dims, preferred_element_type=jnp.float32)
    imag_part = lax.dot_general(weighted_part, crossed, contract_dims, preferred_element_type=jnp.float32)
    return jnp.stack([real_part, imag_part])

def reference(valence, conduction, valence_energy, conduction_energy, band_pairs, grid_index):
    spectrum, weights = pair_spectrum(valence, conduction, valence_energy, conduction_energy, band_pairs)
    selected = jnp.take(spectrum, grid_index, axis=2)
    weighted = (weights[None, :, None] * selected).astype(jnp.bfloat16)
    density = selected.astype(jnp.bfloat16)
    crossed = jnp.stack([density[1], -density[0]])
    vector_count = grid_index.shape[0]
    block_width = math.gcd(vector_count, 1024)
    pair_count = weighted.shape[1]
    pieces = weighted.reshape(2, pair_count, vector_count // block_width, block_width).transpose(2, 0, 1, 3)

    def one_block(row_block):
        return contract(row_block, density, crossed)
    result = lax.map(one_block, pieces)
    return result.transpose(1, 0, 2, 3).reshape(2, vector_count, vector_count)
```

```python
import math
import numpy as np
import jax
import jax.numpy as jnp
import ml_dtypes
from jax import lax
from jax.sharding import PartitionSpec as P
from jax.experimental import pallas as pl
from jax.experimental.pallas import tpu as pltpu

N1 = N2 = N3 = 32
KA, KB = 256, 128
NGV = 16384
GW = 512


def split_np(t):
    hi = t.astype(ml_dtypes.bfloat16)
    lo = (t - hi.astype(np.float64)).astype(ml_dtypes.bfloat16)
    return hi, lo


def dft_tables():
    a = np.arange(KA)
    r1, r2a = a // 8, a % 8
    ph = (np.outer(r1, r1) / 32.0 + np.outer(r2a, r2a) / 8.0) % 1.0
    c, s = np.cos(2 * np.pi * ph), np.sin(2 * np.pi * ph)
    ta = np.block([[c, s], [-s, c]])
    b = np.arange(KB)
    r2b, r3 = b // 32, b % 32
    ph = (np.outer(r2b, r2b) / 4.0 + np.outer(r3, r3) / 32.0) % 1.0
    c, s = np.cos(2 * np.pi * ph), np.sin(2 * np.pi * ph)
    tb = np.block([[c, s], [-s, c]])
    ph = np.outer(r2a, r2b) / 32.0
    tw = np.stack([np.cos(2 * np.pi * ph), np.sin(2 * np.pi * ph)]).astype(np.float32)
    ta_hi, ta_lo = split_np(ta)
    tb_hi, tb_lo = split_np(tb)
    fold = np.zeros((16, 128), ml_dtypes.bfloat16)
    for p in range(8):
        for ri in range(2):
            fold[ri * 8 + p, p * 16 + ri * 8 : p * 16 + ri * 8 + 8] = 1
    return np.stack([ta_hi, ta_lo]), np.stack([tb_hi, tb_lo]), tw, fold


def split(x):
    hi = x.astype(jnp.bfloat16)
    return hi, (x - hi.astype(jnp.float32)).astype(jnp.bfloat16)


def dot_f32(a, b, dims):
    return lax.dot_general(a, b, (dims, ((), ())), preferred_element_type=jnp.float32)


def spectrum_kernel(v_ref, c_ref, scale_ref, index_ref, ta_ref, tb_ref, tw_ref, fold_ref, y_ref, rr, ri, xt):
    def products(a, _):
        lanes = pl.ds(pl.multiple_of(a * 128, 128), 128)
        vr, vi = v_ref[0, :, lanes].astype(jnp.float32), v_ref[1, :, lanes].astype(jnp.float32)
        cr, ci = c_ref[0, :, lanes].astype(jnp.float32), c_ref[1, :, lanes].astype(jnp.float32)
        rows = pl.ds(pl.multiple_of(a * 8, 8), 8)
        rr[rows, :] = vr * cr + vi * ci
        ri[rows, :] = vr * ci - vi * cr
        return 0

    lax.fori_loop(0, KA, products, 0, unroll=8)

    nn = ((1,), (0,))
    nt = ((1,), (1,))
    for h in range(4):
        x = jnp.concatenate(
            [
                jnp.concatenate([r[pl.ds(2 * h + q, KA, stride=8), :] for q in range(2)], axis=1)
                for r in (rr, ri)
            ],
            axis=0,
        )
        xh, xl = split(x)
        z = dot_f32(ta_ref[0], xh, nn) + (dot_f32(ta_ref[0], xl, nn) + dot_f32(ta_ref[1], xh, nn))
        for q in range(2):
            p = 2 * h + q
            zr, zi = z[:KA, q * KB : (q + 1) * KB], z[KA:, q * KB : (q + 1) * KB]
            t = jnp.concatenate([zr * tw_ref[0] + zi * tw_ref[1], zi * tw_ref[0] - zr * tw_ref[1]], axis=1)
            th, tl = split(t)
            s = dot_f32(tb_ref[0], th, nt) + (dot_f32(tb_ref[0], tl, nt) + dot_f32(tb_ref[1], th, nt))
            xt[p] = (s * scale_ref[p]).astype(jnp.bfloat16)

    def select(w, _):
        k = index_ref[pl.ds(w, 1), :]
        ka = (k >> 10) * 8 + ((k >> 5) & 7)
        kb = ((k >> 8) & 3) * 32 + (k & 31)
        hot = jnp.where(lax.broadcasted_iota(jnp.int32, (KA, GW), 0) == ka, 1.0, 0.0).astype(jnp.bfloat16)
        kb_hi = jnp.broadcast_to(kb >> 3, (8, GW))
        low = lax.broadcasted_iota(jnp.int32, (8, GW), 0) == (kb & 7)
        parts = []
        for p in range(8):
            r = jnp.dot(xt[p], hot, preferred_element_type=jnp.float32)
            for q in range(2):
                acc = r[q * KB : q * KB + 8]
                for j in range(1, 16):
                    acc = jnp.where(kb_hi == j, r[q * KB + j * 8 : q * KB + j * 8 + 8], acc)
                parts.append(jnp.where(low, acc, 0.0))
        part = jnp.concatenate(parts, axis=0).astype(jnp.bfloat16)
        y = jnp.dot(fold_ref[...], part, preferred_element_type=jnp.float32)
        y_ref[:, pl.ds(pl.multiple_of(w * GW, GW), GW)] = y.astype(jnp.bfloat16)
        return 0

    lax.fori_loop(0, NGV // GW, select, 0)


def spectrum(v_rows, c_rows, scale, index):
    ta, tb, tw, fold = dft_tables()
    vm = pl.BlockSpec(memory_space=pltpu.VMEM)
    return pl.pallas_call(
        spectrum_kernel,
        out_shape=jax.ShapeDtypeStruct((16, NGV), jnp.bfloat16),
        in_specs=[vm, vm, pl.BlockSpec(memory_space=pltpu.SMEM)] + [vm] * 5,
        out_specs=vm,
        scratch_shapes=[
            pltpu.VMEM((8 * KA, 128), jnp.float32),
            pltpu.VMEM((8 * KA, 128), jnp.float32),
            pltpu.VMEM((8, 256, 256), jnp.bfloat16),
        ],
        compiler_params=pltpu.CompilerParams(vmem_limit_bytes=48 << 20),
        name="spectrum",
    )(v_rows, c_rows, scale, index.reshape(NGV // GW, GW), jnp.asarray(ta), jnp.asarray(tb), jnp.asarray(tw), jnp.asarray(fold))


MESH = pl.DeviceIdType.MESH
ROWS, COLS = 8, 16
GA, GB = NGV // ROWS, NGV // COLS
HALF, PART = GA // 2, GA // 4


def exchange_kernel(y_ref, a_ref, b_ref, pa, at, send, recv, local):
    row, col = lax.axis_index("row"), lax.axis_index("col")
    x, core = row // 2, row % 2
    py, pz = col // 4, col % 4

    def cell(dy, dz):
        return lax.rem(py + dy + 4, 4) * 4 + lax.rem(pz + dz + 4, 4)

    def line(dx, dc=0):
        return lax.rem(x + dx + 4, 4) * 2 + lax.rem(core + dc, 2)

    started = []

    def remote(k, src, dst, device):
        copy = pltpu.make_async_remote_copy(
            src_ref=src, dst_ref=dst, send_sem=send.at[k], recv_sem=recv.at[k],
            device_id=device, device_id_type=MESH,
        )
        copy.start()
        started.append(copy)

    def arrived(k, dst):
        pltpu.make_async_remote_copy(
            src_ref=dst, dst_ref=dst, send_sem=send.at[k], recv_sem=recv.at[k],
            device_id=(row, col), device_id_type=MESH,
        ).wait_recv()

    barrier = pltpu.get_barrier_semaphore()
    for d in range(1, ROWS):
        pl.semaphore_signal(barrier, inc=1, device_id=(lax.rem(row + d, ROWS), col), device_id_type=MESH)
    for d in range(1, COLS):
        pl.semaphore_signal(barrier, inc=1, device_id=(row, lax.rem(col + d, COLS)), device_id_type=MESH)
    pl.semaphore_wait(barrier, ROWS + COLS - 2)

    def a_cols(i):
        return y_ref.at[:, pl.ds(pl.multiple_of(i * GA, GA), GA)]

    def b_cols(j):
        return y_ref.at[:, pl.ds(pl.multiple_of(j * GB, GB), GB)]

    own_a = pltpu.make_async_copy(a_cols(row), pa.at[row], local.at[0])
    own_a.start()
    for d in range(1, ROWS):
        to = lax.rem(row + d, ROWS)
        remote(d - 1, a_cols(to), pa.at[row], (to, col))
    own_b = pltpu.make_async_copy(b_cols(col), b_ref.at[row, col], local.at[1])
    own_b.start()
    base_b0 = 7
    for d in range(1, COLS):
        to = lax.rem(col + d, COLS)
        remote(base_b0 + d - 1, b_cols(to), b_ref.at[row, col], (row, to))

    own_a.wait()
    for d in range(1, ROWS):
        arrived(d - 1, pa.at[lax.rem(row - d + ROWS, ROWS)])

    base_a = (22, 42)

    def turn(h):
        def step(n, _):
            cols = pl.ds(pl.multiple_of(h * HALF + n * 128, 128), 128)
            block = pa[:, :, cols].reshape(128, 128)
            at[cols, :] = block.astype(jnp.float32).T.astype(jnp.bfloat16)
            return 0

        lax.fori_loop(0, HALF // 128, step, 0)

    def near(h, s, d):
        on_y = (h == 0) == (s == 0)
        return cell(d, 0) if on_y else cell(0, d)

    def offset(h, u, d):
        return cell(u, d) if h == 0 else cell(d, u)

    def rows_of(h, part=None):
        if part is None:
            return pl.ds(h * HALF, HALF)
        return pl.ds(h * HALF + part * PART, PART)

    def chunk(h, j, part=None):
        return a_ref.at[j, rows_of(h, part)]

    own_copies = []
    for h in range(2):
        turn(h)
        mine = at.at[rows_of(h)]
        for n, d in ((0, 1), (1, -1)):
            remote(base_a[h] + n, mine, chunk(h, col), (row, near(h, 0, d)))
        copy = pltpu.make_async_copy(mine, chunk(h, col), local.at[2 + h])
        copy.start()
        own_copies.append(copy)

    def second(h, slot, u):
        j = offset(h, u, 0)
        src = at.at[rows_of(h)] if u == 0 else chunk(h, j)
        for n, d in ((0, 1), (1, -1)):
            remote(base_a[h] + 4 + slot * 4 + n, src, chunk(h, j), (row, near(h, 1, d)))

    for h in range(2):
        second(h, 0, 0)

    base_b1 = 62
    own_b.wait()
    for d in range(1, COLS):
        arrived(base_b0 + d - 1, b_ref.at[row, lax.rem(col - d + COLS, COLS)])
    remote(base_b1 + 0, b_ref.at[row], b_ref.at[row], (line(1), col))
    remote(base_b1 + 1, b_ref.at[row], b_ref.at[row], (line(-1), col))
    remote(base_b1 + 2, b_ref.at[row], b_ref.at[row], (line(0, 1), col))

    def b_part(i, part):
        return b_ref.at[i, pl.ds(part * 8, 8)]

    for n, d in ((0, -1), (1, 1)):
        for h in range(2):
            j = offset(h, d, 0)
            arrived(base_a[h] + n, chunk(h, j))
            remote(base_a[h] + 2 + n, chunk(h, j, n), chunk(h, j, n), (row, near(h, 0, -d)))
            second(h, 1 + n, d)

    for n, d in ((0, -1), (1, 1)):
        i = line(d)
        arrived(base_b1 + n, b_ref.at[i])
        remote(base_b1 + 3 + n, b_part(i, n), b_part(i, n), (line(-d), col))
        remote(base_b1 + 5 + n, b_ref.at[i], b_ref.at[i], (line(0, 1), col))

    for h in range(2):
        j = offset(h, 2, 0)
        for n in range(2):
            arrived(base_a[h] + 2 + n, chunk(h, j, n))
        second(h, 3, 2)

    for n in range(2):
        arrived(base_b1 + 3 + n, b_part(line(2), n))
        remote(base_b1 + 7 + n, b_part(line(2), n), b_part(line(2), n), (line(0, 1), col))

    for slot, u in enumerate((0, -1, 1, 2)):
        for n, d in ((0, -1), (1, 1)):
            for h in range(2):
                j = offset(h, u, d)
                k = base_a[h] + 4 + slot * 4
                arrived(k + n, chunk(h, j))
                remote(k + 2 + n, chunk(h, j, n), chunk(h, j, n), (row, near(h, 1, -d)))
    for slot, u in enumerate((0, -1, 1, 2)):
        for n in range(2):
            for h in range(2):
                arrived(base_a[h] + 4 + slot * 4 + 2 + n, chunk(h, offset(h, u, 2), n))

    arrived(base_b1 + 2, b_ref.at[line(0, 1)])
    for n, d in ((0, -1), (1, 1)):
        arrived(base_b1 + 5 + n, b_ref.at[line(d, 1)])
        arrived(base_b1 + 7 + n, b_part(line(2, 1), n))
    for copy in own_copies:
        copy.wait()
    for copy in started:
        copy.wait_send()


def exchange(y):
    anywhere = pl.BlockSpec(memory_space=pl.ANY)
    return pl.pallas_call(
        exchange_kernel,
        out_shape=(
            jax.ShapeDtypeStruct((COLS, GA, 128), jnp.bfloat16),
            jax.ShapeDtypeStruct((ROWS, COLS, 16, GB), jnp.bfloat16),
        ),
        in_specs=[anywhere],
        out_specs=(anywhere, anywhere),
        scratch_shapes=[
            pltpu.VMEM((ROWS, 16, GA), jnp.bfloat16),
            pltpu.VMEM((GA, 128), jnp.bfloat16),
            pltpu.SemaphoreType.DMA((71,)),
            pltpu.SemaphoreType.DMA((71,)),
            pltpu.SemaphoreType.DMA((4,)),
        ],
        compiler_params=pltpu.CompilerParams(collective_id=0, has_side_effects=True),
        name="exchange",
    )(y)


TM = 256


def response_kernel(a_ref, b_ref, o_ref, rhs):
    @pl.when(pl.program_id(0) == 0)
    def _():
        def build(n, _):
            i, j = n // COLS, lax.rem(n, COLS)
            block = b_ref[i, j].astype(jnp.float32)
            re, im = block[:8], block[8:]
            rows = pl.ds(pl.multiple_of(j * 128 + i * 16, 16), 16)
            rhs[rows, :GB] = (-block).astype(jnp.bfloat16)
            rhs[rows, GB:] = jnp.concatenate([-im, re], axis=0).astype(jnp.bfloat16)
            return 0

        lax.fori_loop(0, ROWS * COLS, build, 0)

    lhs = jnp.concatenate([a_ref[j] for j in range(COLS)], axis=1)
    for q in range(2):
        o_ref[q] = jnp.dot(lhs, rhs[:, q * GB : (q + 1) * GB], preferred_element_type=jnp.float32)


def contract(a, b):
    return pl.pallas_call(
        response_kernel,
        out_shape=jax.ShapeDtypeStruct((2, GA, GB), jnp.float32),
        grid=(GA // TM,),
        in_specs=[
            pl.BlockSpec((COLS, TM, 128), lambda m: (0, m, 0)),
            pl.BlockSpec((ROWS, COLS, 16, GB), lambda m: (0, 0, 0, 0), pipeline_mode=pl.Buffered(1)),
        ],
        out_specs=pl.BlockSpec((2, TM, GB), lambda m: (0, m, 0)),
        scratch_shapes=[pltpu.VMEM((COLS * 128, 2 * GB), jnp.bfloat16)],
        compiler_params=pltpu.CompilerParams(vmem_limit_bytes=48 << 20),
        name="contract",
    )(a, b)


def body(valence, conduction, valence_energy, conduction_energy, band_pairs, grid_index):
    v, c = band_pairs[:, 0], band_pairs[:, 1]
    v_rows = jnp.take(valence, v, axis=1, mode="clip")
    c_rows = jnp.take(conduction, c, axis=1, mode="clip")
    gap = jnp.take(valence_energy, v, mode="clip") - jnp.take(conduction_energy, c, mode="clip")
    scale = jnp.sqrt(-2.0 / (math.sqrt(1024) * gap)) / math.sqrt(N1 * N2 * N3)
    y = spectrum(v_rows, c_rows, scale, grid_index)
    a, b = exchange(y)
    return contract(a, b)


def solution(mesh):
    return jax.shard_map(
        body,
        mesh=mesh,
        in_specs=(P(), P(), P(), P(), P(("row", "col"), None), P()),
        out_specs=P(None, "row", "col"),
        check_vma=False,
    )
```

```python
import math
import numpy as np
import jax
import jax.numpy as jnp
import ml_dtypes
from jax import lax
from jax.sharding import PartitionSpec as P
from jax.experimental import pallas as pl
from jax.experimental.pallas import tpu as pltpu

N1 = N2 = N3 = 32
KA, KB = 256, 128
NGV = 16384
GW = 1024


def split_np(t):
    hi = t.astype(ml_dtypes.bfloat16)
    lo = (t - hi.astype(np.float64)).astype(ml_dtypes.bfloat16)
    return hi, lo


def dft_tables():
    a = np.arange(KA)
    r1, r2a = a // 8, a % 8
    ph = (np.outer(r1, r1) / 32.0 + np.outer(r2a, r2a) / 8.0) % 1.0
    c, s = np.cos(2 * np.pi * ph), np.sin(2 * np.pi * ph)
    ta = np.block([[c, s], [-s, c]])
    b = np.arange(KB)
    r2b, r3 = b // 32, b % 32
    ph = (np.outer(r2b, r2b) / 4.0 + np.outer(r3, r3) / 32.0) % 1.0
    c, s = np.cos(2 * np.pi * ph), np.sin(2 * np.pi * ph)
    tb = np.block([[c, s], [-s, c]])
    ph = np.outer(r2a, r2b) / 32.0
    tw = np.stack([np.cos(2 * np.pi * ph), np.sin(2 * np.pi * ph)]).astype(np.float32)
    ta_hi, ta_lo = split_np(ta)
    tb_hi, tb_lo = split_np(tb)
    fold = np.zeros((16, 128), ml_dtypes.bfloat16)
    for p in range(8):
        for ri in range(2):
            fold[ri * 8 + p, p * 16 + ri * 8 : p * 16 + ri * 8 + 8] = 1
    return np.stack([ta_hi, ta_lo]), np.stack([tb_hi, tb_lo]), tw, fold


def split(x):
    hi = x.astype(jnp.bfloat16)
    return hi, (x - hi.astype(jnp.float32)).astype(jnp.bfloat16)


def dot_f32(a, b, dims):
    return lax.dot_general(a, b, (dims, ((), ())), preferred_element_type=jnp.float32)


def spectrum_kernel(v_ref, c_ref, scale_ref, ta_ref, tb_ref, tw_ref, xt, rr, ri):
    def products(a, _):
        lanes = pl.ds(pl.multiple_of(a * 128, 128), 128)
        vr, vi = v_ref[0, :, lanes].astype(jnp.float32), v_ref[1, :, lanes].astype(jnp.float32)
        cr, ci = c_ref[0, :, lanes].astype(jnp.float32), c_ref[1, :, lanes].astype(jnp.float32)
        rows = pl.ds(pl.multiple_of(a * 8, 8), 8)
        rr[rows, :] = vr * cr + vi * ci
        ri[rows, :] = vr * ci - vi * cr
        return 0

    lax.fori_loop(0, KA, products, 0, unroll=8)

    nn = ((1,), (0,))
    nt = ((1,), (1,))
    for h in range(4):
        x = jnp.concatenate(
            [
                jnp.concatenate([r[pl.ds(2 * h + q, KA, stride=8), :] for q in range(2)], axis=1)
                for r in (rr, ri)
            ],
            axis=0,
        )
        xh, xl = split(x)
        z = dot_f32(ta_ref[0], xh, nn) + (dot_f32(ta_ref[0], xl, nn) + dot_f32(ta_ref[1], xh, nn))
        for q in range(2):
            p = 2 * h + q
            zr, zi = z[:KA, q * KB : (q + 1) * KB], z[KA:, q * KB : (q + 1) * KB]
            t = jnp.concatenate([zr * tw_ref[0] + zi * tw_ref[1], zi * tw_ref[0] - zr * tw_ref[1]], axis=1)
            th, tl = split(t)
            s = dot_f32(tb_ref[0], th, nt) + (dot_f32(tb_ref[0], tl, nt) + dot_f32(tb_ref[1], th, nt))
            xt[p] = (s * scale_ref[p]).astype(jnp.bfloat16)

def spectrum(v_rows, c_rows, scale):
    ta, tb, tw, _ = dft_tables()
    vm = pl.BlockSpec(memory_space=pltpu.VMEM)
    return pl.pallas_call(
        spectrum_kernel,
        out_shape=jax.ShapeDtypeStruct((8, 256, 256), jnp.bfloat16),
        in_specs=[vm, vm, pl.BlockSpec(memory_space=pltpu.SMEM)] + [vm] * 3,
        out_specs=vm,
        scratch_shapes=[pltpu.VMEM((8 * KA, 128), jnp.float32)] * 2,
        compiler_params=pltpu.CompilerParams(vmem_limit_bytes=32 << 20),
        name="spectrum",
    )(v_rows, c_rows, scale, jnp.asarray(ta), jnp.asarray(tb), jnp.asarray(tw))


MESH = pl.DeviceIdType.MESH
ROWS, COLS = 8, 16
GA, GB = NGV // ROWS, NGV // COLS
SUB, SW = 4, 512
HALF, PART = SW // 2, SW // 4
STEPS = 28


def exchange_kernel(
    xt, index_ref, fold_ref, a_ref, b_ref, ys, pa, at,
    a0s, a0r, b0s, b0r, a1s, a1r, b1s, b1r, own_a, own_b, own_t,
):
    row, col = lax.axis_index("row"), lax.axis_index("col")
    x, core = row // 2, row % 2
    py, pz = col // 4, col % 4

    def cell(dy, dz):
        return lax.rem(py + dy + 4, 4) * 4 + lax.rem(pz + dz + 4, 4)

    def line(dx, dc=0):
        return lax.rem(x + dx + 4, 4) * 2 + lax.rem(core + dc, 2)

    def remote(src, dst, send, recv, device):
        return pltpu.make_async_remote_copy(
            src_ref=src, dst_ref=dst, send_sem=send, recv_sem=recv,
            device_id=device, device_id_type=MESH,
        )

    barrier = pltpu.get_barrier_semaphore()
    for d in range(1, ROWS):
        pl.semaphore_signal(barrier, inc=1, device_id=(lax.rem(row + d, ROWS), col), device_id_type=MESH)
    for d in range(1, COLS):
        pl.semaphore_signal(barrier, inc=1, device_id=(row, lax.rem(col + d, COLS)), device_id_type=MESH)
    pl.semaphore_wait(barrier, ROWS + COLS - 2)


    def select(s, m):
        k = jnp.concatenate([index_ref[pl.ds((2 * m + e) * SUB + s, 1), :] for e in range(2)], axis=1)
        ka = (k >> 10) * 8 + ((k >> 5) & 7)
        kb = ((k >> 8) & 3) * 32 + (k & 31)
        hot = jnp.where(lax.broadcasted_iota(jnp.int32, (KA, GW), 0) == ka, 1.0, 0.0).astype(jnp.bfloat16)
        kb_hi = jnp.broadcast_to(kb >> 3, (8, GW))
        low = lax.broadcasted_iota(jnp.int32, (8, GW), 0) == (kb & 7)
        parts = []
        for p in range(8):
            r = jnp.dot(xt[p], hot, preferred_element_type=jnp.float32)
            for q in range(2):
                acc = r[q * KB : q * KB + 8]
                for j in range(1, 16):
                    acc = jnp.where(kb_hi == j, r[q * KB + j * 8 : q * KB + j * 8 + 8], acc)
                parts.append(jnp.where(low, acc, 0.0))
        part = jnp.concatenate(parts, axis=0).astype(jnp.bfloat16)
        y = jnp.dot(fold_ref[...], part, preferred_element_type=jnp.float32).astype(jnp.bfloat16)
        for e in range(2):
            ys[s, 2 * m + e] = y[:, e * SW : (e + 1) * SW]


    def a0(s, i):
        return remote(ys.at[s, i], pa.at[s, row], a0s.at[s, i], a0r.at[s, row], (i, col))

    def b0(s, i):
        j = 2 * i + s // 2
        return remote(ys.at[s, i], b_ref.at[row, s % 2, col], b0s.at[s, i], b0r.at[s % 2, col], (row, j))

    def keep_a(s):
        return pltpu.make_async_copy(ys.at[s, row], pa.at[s, row], own_a.at[s])

    def keep_b(s):
        return pltpu.make_async_copy(ys.at[s, col // 2], b_ref.at[row, s % 2, col], own_b.at[s % 2])

    def hand_out(s, m):
        for e in range(2):
            i = 2 * m + e

            @pl.when(i != row)
            def _():
                a0(s, i).start()

            @pl.when(i == row)
            def _():
                keep_a(s).start()

            @pl.when(2 * i + s // 2 != col)
            def _():
                b0(s, i).start()

            @pl.when(2 * i + s // 2 == col)
            def _():
                keep_b(s).start()


    def along(h, first, d):
        return (row, cell(d, 0) if (h == 0) == first else cell(0, d))

    def spot(h, u, d):
        return cell(u, d) if h == 0 else cell(d, u)

    def rows(s, h, part=None):
        if part is None:
            return pl.ds(pl.multiple_of(s * SW + h * HALF, HALF), HALF)
        return pl.ds(pl.multiple_of(s * SW + h * HALF + part * PART, PART), PART)

    def a1(s, h, k, j, device, part=None, src=None):
        dst = a_ref.at[j, rows(s, h, part)]
        return remote(dst if src is None else src, dst, a1s.at[s, h, k], a1r.at[s, h, k], device)

    SIDES = ((0, 1), (1, -1))

    def second(s, h, slot, u):
        src = at.at[rows(s, h)] if u == 0 else None
        for n, d in SIDES:
            a1(s, h, 4 + slot * 4 + n, spot(h, u, 0), along(h, False, d), src=src).start()

    def keep_t(s):
        span = pl.ds(pl.multiple_of(s * SW, SW), SW)
        return pltpu.make_async_copy(at.at[span], a_ref.at[col, span], own_t.at[s])

    def turn(s):
        keep_a(s).wait()
        for d in range(1, ROWS):
            src = lax.rem(row + d, ROWS)
            remote(ys.at[s, row], pa.at[s, src], a0s.at[s, src], a0r.at[s, src], (src, col)).wait_recv()
        for n in range(SW // 128):
            block = pa[s, :, :, n * 128 : (n + 1) * 128].reshape(128, 128)
            span = pl.ds(pl.multiple_of(s * SW + n * 128, 128), 128)
            at[span, :] = block.astype(jnp.float32).T.astype(jnp.bfloat16)
        for h in range(2):
            for n, d in SIDES:
                a1(s, h, n, col, along(h, True, d), src=at.at[rows(s, h)]).start()
        keep_t(s).start()
        for h in range(2):
            second(s, h, 0, 0)

    def near(s):
        for n, d in SIDES:
            for h in range(2):
                j = spot(h, -d, 0)
                a1(s, h, n, j, (row, col)).wait_recv()
                a1(s, h, 2 + n, j, along(h, True, d), part=n).start()
                second(s, h, 1 + n, -d)

    def far(s):
        for h in range(2):
            for n in range(2):
                a1(s, h, 2 + n, spot(h, 2, 0), (row, col), part=n).wait_recv()
            second(s, h, 3, 2)

    SLOTS = ((0, 0), (1, -1), (2, 1), (3, 2))

    def pass_on(s, slot, u):
        for n, d in SIDES:
            for h in range(2):
                j = spot(h, u, -d)
                k = 4 + slot * 4 + n
                a1(s, h, k, j, (row, col)).wait_recv()
                a1(s, h, k + 2, j, along(h, False, d), part=n).start()

    def last(s, _):
        for slot, u in SLOTS:
            for n in range(2):
                for h in range(2):
                    a1(s, h, 6 + slot * 4 + n, spot(h, u, 2), (row, col), part=n).wait_recv()
        return 0


    def b1(f, k, i, device, part=None):
        ref = b_ref.at[i, f] if part is None else b_ref.at[i, f, pl.ds(part * 8, 8)]
        return remote(ref, ref, b1s.at[f, k], b1r.at[f, k], device)

    def sides(f):
        s = (col % 2) * 2 + f
        keep_b(s).wait()
        for d in range(1, COLS):
            src = lax.rem(col + d, COLS)
            remote(ys.at[s, 0], b_ref.at[row, f, src], b0s.at[s, 0], b0r.at[f, src], (row, src)).wait_recv()
        for n, d in SIDES:
            b1(f, n, row, (line(d), col)).start()
        b1(f, 2, row, (line(0, 1), col)).start()

    def sides_near(f):
        for n, d in SIDES:
            i = line(-d)
            b1(f, n, i, (row, col)).wait_recv()
            b1(f, 3 + n, i, (line(d), col), part=n).start()
            b1(f, 5 + n, i, (line(0, 1), col)).start()

    def sides_far(f):
        for n in range(2):
            b1(f, 3 + n, line(2), (row, col), part=n).wait_recv()
            b1(f, 7 + n, line(2), (line(0, 1), col), part=n).start()

    def sides_last(f, _):
        b1(f, 2, line(0, 1), (row, col)).wait_recv()
        for n, d in SIDES:
            b1(f, 5 + n, line(-d, 1), (row, col)).wait_recv()
            b1(f, 7 + n, line(2, 1), (row, col), part=n).wait_recv()
        return 0

    def step(n, _):
        @pl.when(n < 4 * SUB)
        def _():
            select(n // 4, n % 4)
            hand_out(n // 4, n % 4)

        def event(delay, run):
            s = (n - delay) // 4

            @pl.when((n >= delay) & (n < delay + 4 * SUB) & ((n - delay) % 4 == 0))
            def _():
                run(s)

        def column_event(delay, run):
            s = (n - delay) // 4

            @pl.when((n >= delay) & (n < delay + 4 * SUB) & ((n - delay) % 4 == 0) & (s // 2 == col % 2))
            def _():
                run(s % 2)

        event(5, turn)
        event(7, near)
        event(9, far)
        event(8, lambda s: pass_on(s, 0, 0))
        event(10, lambda s: pass_on(s, 1, -1))
        event(11, lambda s: pass_on(s, 2, 1))
        event(12, lambda s: pass_on(s, 3, 2))
        column_event(6, sides)
        column_event(10, sides_near)
        column_event(13, sides_far)
        return 0

    lax.fori_loop(0, STEPS, step, 0)
    lax.fori_loop(0, SUB, last, 0)
    lax.fori_loop(0, 2, sides_last, 0)


    def sent(s, _):
        keep_t(s).wait()
        for i in range(ROWS):
            @pl.when(i != row)
            def _():
                a0(s, i).wait_send()

            @pl.when(2 * i + s // 2 != col)
            def _():
                b0(s, i).wait_send()

        for h in range(2):
            for k in (0, 1) + tuple(4 + t * 4 + n for t in range(4) for n in range(2)):
                a1(s, h, k, col, (row, col)).wait_send()
                a1(s, h, k + 2, col, (row, col), part=0).wait_send()
        return 0

    def column_sent(f, _):
        for k in (0, 1, 2, 5, 6):
            b1(f, k, row, (row, col)).wait_send()
        for k in (3, 4, 7, 8):
            b1(f, k, row, (row, col), part=0).wait_send()
        return 0

    lax.fori_loop(0, SUB, sent, 0)
    lax.fori_loop(0, 2, column_sent, 0)


def exchange(xt, index):
    anywhere, vm = pl.BlockSpec(memory_space=pl.ANY), pl.BlockSpec(memory_space=pltpu.VMEM)
    dma = pltpu.SemaphoreType.DMA
    return pl.pallas_call(
        exchange_kernel,
        out_shape=(
            jax.ShapeDtypeStruct((COLS, GA, 128), jnp.bfloat16),
            jax.ShapeDtypeStruct((ROWS, 2, COLS, 16, SW), jnp.bfloat16),
        ),
        in_specs=[vm, vm, vm],
        out_specs=(anywhere, anywhere),
        scratch_shapes=[
            pltpu.VMEM((SUB, ROWS, 16, SW), jnp.bfloat16),
            pltpu.VMEM((SUB, ROWS, 16, SW), jnp.bfloat16),
            pltpu.VMEM((GA, 128), jnp.bfloat16),
            dma((SUB, ROWS)), dma((SUB, ROWS)),
            dma((SUB, ROWS)), dma((2, COLS)),
            dma((SUB, 2, 20)), dma((SUB, 2, 20)),
            dma((2, 9)), dma((2, 9)),
            dma((SUB,)), dma((2,)), dma((SUB,)),
        ],
        compiler_params=pltpu.CompilerParams(
            collective_id=0, has_side_effects=True, vmem_limit_bytes=32 << 20
        ),
        name="exchange",
    )(xt, index.reshape(ROWS * SUB, SW), jnp.asarray(dft_tables()[3]))


TM = 256


def response_kernel(a_ref, b_ref, o_ref, rhs):
    @pl.when(pl.program_id(0) == 0)
    def _():
        def build(n, _):
            i, j = n // COLS, lax.rem(n, COLS)
            block = jnp.concatenate([b_ref[i, f, j] for f in range(2)], axis=1).astype(jnp.float32)
            re, im = block[:8], block[8:]
            rows = pl.ds(pl.multiple_of(j * 128 + i * 16, 16), 16)
            rhs[rows, :GB] = (-block).astype(jnp.bfloat16)
            rhs[rows, GB:] = jnp.concatenate([-im, re], axis=0).astype(jnp.bfloat16)
            return 0

        lax.fori_loop(0, ROWS * COLS, build, 0)

    lhs = jnp.concatenate([a_ref[j] for j in range(COLS)], axis=1)
    for q in range(2):
        o_ref[q] = jnp.dot(lhs, rhs[:, q * GB : (q + 1) * GB], preferred_element_type=jnp.float32)


def contract(a, b):
    return pl.pallas_call(
        response_kernel,
        out_shape=jax.ShapeDtypeStruct((2, GA, GB), jnp.float32),
        grid=(GA // TM,),
        in_specs=[
            pl.BlockSpec((COLS, TM, 128), lambda m: (0, m, 0)),
            pl.BlockSpec((ROWS, 2, COLS, 16, SW), lambda m: (0, 0, 0, 0, 0), pipeline_mode=pl.Buffered(1)),
        ],
        out_specs=pl.BlockSpec((2, TM, GB), lambda m: (0, m, 0)),
        scratch_shapes=[pltpu.VMEM((COLS * 128, 2 * GB), jnp.bfloat16)],
        compiler_params=pltpu.CompilerParams(vmem_limit_bytes=48 << 20),
        name="contract",
    )(a, b)


def body(valence, conduction, valence_energy, conduction_energy, band_pairs, grid_index):
    v, c = band_pairs[:, 0], band_pairs[:, 1]
    v_rows = jnp.take(valence, v, axis=1, mode="clip")
    c_rows = jnp.take(conduction, c, axis=1, mode="clip")
    gap = jnp.take(valence_energy, v, mode="clip") - jnp.take(conduction_energy, c, mode="clip")
    scale = jnp.sqrt(-2.0 / (math.sqrt(1024) * gap)) / math.sqrt(N1 * N2 * N3)
    a, b = exchange(spectrum(v_rows, c_rows, scale), grid_index)
    return contract(a, b)


def solution(mesh):
    return jax.shard_map(
        body,
        mesh=mesh,
        in_specs=(P(), P(), P(), P(), P(("row", "col"), None), P()),
        out_specs=P(None, "row", "col"),
        check_vma=False,
    )
```

```python
import math
import numpy as np
import jax
import jax.numpy as jnp
import ml_dtypes
from jax import lax
from jax.sharding import PartitionSpec as P
from jax.experimental import pallas as pl
from jax.experimental.pallas import tpu as pltpu

N1 = N2 = N3 = 32
KA, KB = 256, 128
NGV = 16384
NR = 32768
GW = 1024


def split_np(t):
    hi = t.astype(ml_dtypes.bfloat16)
    lo = (t - hi.astype(np.float64)).astype(ml_dtypes.bfloat16)
    return hi, lo


def dft_tables():
    a = np.arange(KA)
    r1, r2a = a // 8, a % 8
    ph = (np.outer(r1, r1) / 32.0 + np.outer(r2a, r2a) / 8.0) % 1.0
    c, s = np.cos(2 * np.pi * ph), np.sin(2 * np.pi * ph)
    ta = np.block([[c, s], [-s, c]])
    b = np.arange(KB)
    r2b, r3 = b // 32, b % 32
    ph = (np.outer(r2b, r2b) / 4.0 + np.outer(r3, r3) / 32.0) % 1.0
    c, s = np.cos(2 * np.pi * ph), np.sin(2 * np.pi * ph)
    tb = np.block([[c, s], [-s, c]])
    ph = np.outer(r2a, r2b) / 32.0
    tw = np.stack([np.cos(2 * np.pi * ph), np.sin(2 * np.pi * ph)]).astype(np.float32)
    ta_hi, ta_lo = split_np(ta)
    tb_hi, tb_lo = split_np(tb)
    fold = np.zeros((16, 128), ml_dtypes.bfloat16)
    for p in range(8):
        for ri in range(2):
            fold[ri * 8 + p, p * 16 + ri * 8 : p * 16 + ri * 8 + 8] = 1
    return np.stack([ta_hi, ta_lo]), np.stack([tb_hi, tb_lo]), tw, fold


def split(x):
    hi = x.astype(jnp.bfloat16)
    return hi, (x - hi.astype(jnp.float32)).astype(jnp.bfloat16)


def dot_f32(a, b, dims):
    return lax.dot_general(a, b, (dims, ((), ())), preferred_element_type=jnp.float32)


def spectrum_kernel(
    bands, v_energy, c_energy, valence, conduction, ta_hbm, tb_hbm, tw_hbm, xt,
    v_half, c_half, v_full, c_full, ta, tb, tw, sems,
):
    tables = [
        pltpu.make_async_copy(src, dst, sems.at[k])
        for k, (src, dst) in enumerate(((valence, v_half), (ta_hbm, ta), (tb_hbm, tb), (tw_hbm, tw)))
    ]

    def strip(p):
        rows = pl.ds(pl.multiple_of(bands[p, 1] // 8 * 8, 8), 8)
        return pltpu.make_async_copy(conduction.at[:, rows, :], c_half.at[p], sems.at[4 + p])

    tables[0].start()
    strip(0).start()
    strip(1).start()
    for copy in tables[1:]:
        copy.start()
    for p in range(2, 8):
        strip(p).start()

    tables[0].wait()

    def widen_v(a, _):
        lanes = pl.ds(pl.multiple_of(a * 128, 128), 128)
        rows = pl.ds(pl.multiple_of(a * 16, 16), 16)
        for q in range(2):
            v_full[q, rows, :] = v_half[q, :, lanes].astype(jnp.float32)
        return 0

    lax.fori_loop(0, KA, widen_v, 0, unroll=8)

    nn = ((1,), (0,))
    nt = ((1,), (1,))
    for h in range(4):
        for e in range(2):
            strip(2 * h + e).wait()

        def widen_c(a, _):
            lanes = pl.ds(pl.multiple_of(a * 128, 128), 128)
            rows = pl.ds(pl.multiple_of(a * 8, 8), 8)
            for e in range(2):
                for q in range(2):
                    c_full[h % 2, e, q, rows, :] = c_half[2 * h + e, q, :, lanes].astype(jnp.float32)
            return 0

        lax.fori_loop(0, KA, widen_c, 0, unroll=8)
        real, imag = [], []
        for e in range(2):
            p = 2 * h + e
            vr, vi = (v_full[q, pl.ds(bands[p, 0], KA, stride=16), :] for q in range(2))
            cr, ci = (c_full[h % 2, e, q, pl.ds(bands[p, 1] % 8, KA, stride=8), :] for q in range(2))
            real.append(vr * cr + vi * ci)
            imag.append(vr * ci - vi * cr)
        x = jnp.concatenate([jnp.concatenate(real, axis=1), jnp.concatenate(imag, axis=1)], axis=0)
        if h == 0:
            for copy in tables[1:]:
                copy.wait()
        xh, xl = split(x)
        z = dot_f32(ta[0], xh, nn) + (dot_f32(ta[0], xl, nn) + dot_f32(ta[1], xh, nn))
        for e in range(2):
            p = 2 * h + e
            zr, zi = z[:KA, e * KB : (e + 1) * KB], z[KA:, e * KB : (e + 1) * KB]
            t = jnp.concatenate([zr * tw[0] + zi * tw[1], zi * tw[0] - zr * tw[1]], axis=1)
            th, tl = split(t)
            s = dot_f32(tb[0], th, nt) + (dot_f32(tb[0], tl, nt) + dot_f32(tb[1], th, nt))
            gap = jnp.full((1, KA), v_energy[bands[p, 0]] - c_energy[bands[p, 1]], jnp.float32)
            scale = jnp.sqrt(-2.0 / (math.sqrt(1024) * gap)) * (1.0 / math.sqrt(N1 * N2 * N3))
            xt[p] = (s * scale).astype(jnp.bfloat16)


def spectrum(valence, conduction, valence_energy, conduction_energy, band_pairs):
    ta, tb, tw, _ = dft_tables()
    anywhere = pl.BlockSpec(memory_space=pl.ANY)
    scalars = pl.BlockSpec(memory_space=pltpu.SMEM)
    bf, f32 = jnp.bfloat16, jnp.float32
    return pl.pallas_call(
        spectrum_kernel,
        out_shape=jax.ShapeDtypeStruct((8, 256, 256), bf),
        in_specs=[scalars] * 3 + [anywhere] * 5,
        out_specs=pl.BlockSpec(memory_space=pltpu.VMEM),
        scratch_shapes=[
            pltpu.VMEM((2, 16, NR), bf),
            pltpu.VMEM((8, 2, 8, NR), bf),
            pltpu.VMEM((2, KA * 16, 128), f32),
            pltpu.VMEM((2, 2, 2, KA * 8, 128), f32),
            pltpu.VMEM(ta.shape, bf),
            pltpu.VMEM(tb.shape, bf),
            pltpu.VMEM(tw.shape, f32),
            pltpu.SemaphoreType.DMA((12,)),
        ],
        compiler_params=pltpu.CompilerParams(vmem_limit_bytes=48 << 20),
        name="spectrum",
    )(band_pairs, valence_energy, conduction_energy, valence, conduction,
      jnp.asarray(ta), jnp.asarray(tb), jnp.asarray(tw))


MESH = pl.DeviceIdType.MESH
ROWS, COLS = 8, 16
GA, GB = NGV // ROWS, NGV // COLS
SUB, SW = 4, 512
HALF, PART = SW // 2, SW // 4
STEPS = 28


def exchange_kernel(
    xt, index_ref, fold_ref, a_ref, b_ref, ys, pa, at,
    a0s, a0r, b0s, b0r, a1s, a1r, b1s, b1r, own_a, own_b, own_t,
):
    row, col = lax.axis_index("row"), lax.axis_index("col")
    x, core = row // 2, row % 2
    py, pz = col // 4, col % 4

    def cell(dy, dz):
        return lax.rem(py + dy + 4, 4) * 4 + lax.rem(pz + dz + 4, 4)

    def line(dx, dc=0):
        return lax.rem(x + dx + 4, 4) * 2 + lax.rem(core + dc, 2)

    def remote(src, dst, send, recv, device):
        return pltpu.make_async_remote_copy(
            src_ref=src, dst_ref=dst, send_sem=send, recv_sem=recv,
            device_id=device, device_id_type=MESH,
        )

    barrier = pltpu.get_barrier_semaphore()
    for d in range(1, ROWS):
        pl.semaphore_signal(barrier, inc=1, device_id=(lax.rem(row + d, ROWS), col), device_id_type=MESH)
    for d in range(1, COLS):
        pl.semaphore_signal(barrier, inc=1, device_id=(row, lax.rem(col + d, COLS)), device_id_type=MESH)
    pl.semaphore_wait(barrier, ROWS + COLS - 2)


    def select(s, m):
        k = jnp.concatenate([index_ref[pl.ds((2 * m + e) * SUB + s, 1), :] for e in range(2)], axis=1)
        ka = (k >> 10) * 8 + ((k >> 5) & 7)
        kb = ((k >> 8) & 3) * 32 + (k & 31)
        hot = jnp.where(lax.broadcasted_iota(jnp.int32, (KA, GW), 0) == ka, 1.0, 0.0).astype(jnp.bfloat16)
        kb_hi = jnp.broadcast_to(kb >> 3, (8, GW))
        low = lax.broadcasted_iota(jnp.int32, (8, GW), 0) == (kb & 7)
        parts = []
        for p in range(8):
            r = jnp.dot(xt[p], hot, preferred_element_type=jnp.float32)
            for q in range(2):
                acc = r[q * KB : q * KB + 8]
                for j in range(1, 16):
                    acc = jnp.where(kb_hi == j, r[q * KB + j * 8 : q * KB + j * 8 + 8], acc)
                parts.append(jnp.where(low, acc, 0.0))
        part = jnp.concatenate(parts, axis=0).astype(jnp.bfloat16)
        y = jnp.dot(fold_ref[...], part, preferred_element_type=jnp.float32).astype(jnp.bfloat16)
        for e in range(2):
            ys[s, 2 * m + e] = y[:, e * SW : (e + 1) * SW]


    def a0(s, i):
        return remote(ys.at[s, i], pa.at[s, row], a0s.at[s, i], a0r.at[s, row], (i, col))

    def b0(s, i):
        j = 2 * i + s // 2
        return remote(ys.at[s, i], b_ref.at[row, s % 2, col], b0s.at[s, i], b0r.at[s % 2, col], (row, j))

    def keep_a(s):
        return pltpu.make_async_copy(ys.at[s, row], pa.at[s, row], own_a.at[s])

    def keep_b(s):
        return pltpu.make_async_copy(ys.at[s, col // 2], b_ref.at[row, s % 2, col], own_b.at[s % 2])

    def hand_out(s, m):
        for e in range(2):
            i = 2 * m + e

            @pl.when(i != row)
            def _():
                a0(s, i).start()

            @pl.when(i == row)
            def _():
                keep_a(s).start()

            @pl.when(2 * i + s // 2 != col)
            def _():
                b0(s, i).start()

            @pl.when(2 * i + s // 2 == col)
            def _():
                keep_b(s).start()


    def along(h, first, d):
        return (row, cell(d, 0) if (h == 0) == first else cell(0, d))

    def spot(h, u, d):
        return cell(u, d) if h == 0 else cell(d, u)

    def rows(s, h, part=None):
        if part is None:
            return pl.ds(pl.multiple_of(s * SW + h * HALF, HALF), HALF)
        return pl.ds(pl.multiple_of(s * SW + h * HALF + part * PART, PART), PART)

    def a1(s, h, k, j, device, part=None, src=None):
        dst = a_ref.at[j, rows(s, h, part)]
        return remote(dst if src is None else src, dst, a1s.at[s, h, k], a1r.at[s, h, k], device)

    SIDES = ((0, 1), (1, -1))

    def second(s, h, slot, u):
        src = at.at[rows(s, h)] if u == 0 else None
        for n, d in SIDES:
            a1(s, h, 4 + slot * 4 + n, spot(h, u, 0), along(h, False, d), src=src).start()

    def keep_t(s):
        span = pl.ds(pl.multiple_of(s * SW, SW), SW)
        return pltpu.make_async_copy(at.at[span], a_ref.at[col, span], own_t.at[s])

    def turn(s):
        keep_a(s).wait()
        for d in range(1, ROWS):
            src = lax.rem(row + d, ROWS)
            remote(ys.at[s, row], pa.at[s, src], a0s.at[s, src], a0r.at[s, src], (src, col)).wait_recv()
        for n in range(SW // 128):
            block = pa[s, :, :, n * 128 : (n + 1) * 128].reshape(128, 128)
            span = pl.ds(pl.multiple_of(s * SW + n * 128, 128), 128)
            at[span, :] = block.astype(jnp.float32).T.astype(jnp.bfloat16)
        for h in range(2):
            for n, d in SIDES:
                a1(s, h, n, col, along(h, True, d), src=at.at[rows(s, h)]).start()
        keep_t(s).start()
        for h in range(2):
            second(s, h, 0, 0)

    def near(s):
        for n, d in SIDES:
            for h in range(2):
                j = spot(h, -d, 0)
                a1(s, h, n, j, (row, col)).wait_recv()
                a1(s, h, 2 + n, j, along(h, True, d), part=n).start()
                second(s, h, 1 + n, -d)

    def far(s):
        for h in range(2):
            for n in range(2):
                a1(s, h, 2 + n, spot(h, 2, 0), (row, col), part=n).wait_recv()
            second(s, h, 3, 2)

    SLOTS = ((0, 0), (1, -1), (2, 1), (3, 2))

    def pass_on(s, slot, u):
        for n, d in SIDES:
            for h in range(2):
                j = spot(h, u, -d)
                k = 4 + slot * 4 + n
                a1(s, h, k, j, (row, col)).wait_recv()
                a1(s, h, k + 2, j, along(h, False, d), part=n).start()

    def last(s, _):
        for slot, u in SLOTS:
            for n in range(2):
                for h in range(2):
                    a1(s, h, 6 + slot * 4 + n, spot(h, u, 2), (row, col), part=n).wait_recv()
        return 0


    def b1(f, k, i, device, part=None):
        ref = b_ref.at[i, f] if part is None else b_ref.at[i, f, pl.ds(part * 8, 8)]
        return remote(ref, ref, b1s.at[f, k], b1r.at[f, k], device)

    def sides(f):
        s = (col % 2) * 2 + f
        keep_b(s).wait()
        for d in range(1, COLS):
            src = lax.rem(col + d, COLS)
            remote(ys.at[s, 0], b_ref.at[row, f, src], b0s.at[s, 0], b0r.at[f, src], (row, src)).wait_recv()
        for n, d in SIDES:
            b1(f, n, row, (line(d), col)).start()
        b1(f, 2, row, (line(0, 1), col)).start()

    def sides_near(f):
        for n, d in SIDES:
            i = line(-d)
            b1(f, n, i, (row, col)).wait_recv()
            b1(f, 3 + n, i, (line(d), col), part=n).start()
            b1(f, 5 + n, i, (line(0, 1), col)).start()

    def sides_far(f):
        for n in range(2):
            b1(f, 3 + n, line(2), (row, col), part=n).wait_recv()
            b1(f, 7 + n, line(2), (line(0, 1), col), part=n).start()

    def sides_last(f, _):
        b1(f, 2, line(0, 1), (row, col)).wait_recv()
        for n, d in SIDES:
            b1(f, 5 + n, line(-d, 1), (row, col)).wait_recv()
            b1(f, 7 + n, line(2, 1), (row, col), part=n).wait_recv()
        return 0

    def step(n, _):
        @pl.when(n < 4 * SUB)
        def _():
            select(n // 4, n % 4)
            hand_out(n // 4, n % 4)

        def event(delay, run):
            s = (n - delay) // 4

            @pl.when((n >= delay) & (n < delay + 4 * SUB) & ((n - delay) % 4 == 0))
            def _():
                run(s)

        def column_event(delay, run):
            s = (n - delay) // 4

            @pl.when((n >= delay) & (n < delay + 4 * SUB) & ((n - delay) % 4 == 0) & (s // 2 == col % 2))
            def _():
                run(s % 2)

        event(5, turn)
        event(7, near)
        event(9, far)
        event(8, lambda s: pass_on(s, 0, 0))
        event(10, lambda s: pass_on(s, 1, -1))
        event(11, lambda s: pass_on(s, 2, 1))
        event(12, lambda s: pass_on(s, 3, 2))
        column_event(6, sides)
        column_event(10, sides_near)
        column_event(13, sides_far)
        return 0

    lax.fori_loop(0, STEPS, step, 0)
    lax.fori_loop(0, SUB, last, 0)
    lax.fori_loop(0, 2, sides_last, 0)


    def sent(s, _):
        keep_t(s).wait()
        for i in range(ROWS):
            @pl.when(i != row)
            def _():
                a0(s, i).wait_send()

            @pl.when(2 * i + s // 2 != col)
            def _():
                b0(s, i).wait_send()

        for h in range(2):
            for k in (0, 1) + tuple(4 + t * 4 + n for t in range(4) for n in range(2)):
                a1(s, h, k, col, (row, col)).wait_send()
                a1(s, h, k + 2, col, (row, col), part=0).wait_send()
        return 0

    def column_sent(f, _):
        for k in (0, 1, 2, 5, 6):
            b1(f, k, row, (row, col)).wait_send()
        for k in (3, 4, 7, 8):
            b1(f, k, row, (row, col), part=0).wait_send()
        return 0

    lax.fori_loop(0, SUB, sent, 0)
    lax.fori_loop(0, 2, column_sent, 0)


def exchange(xt, index):
    anywhere, vm = pl.BlockSpec(memory_space=pl.ANY), pl.BlockSpec(memory_space=pltpu.VMEM)
    dma = pltpu.SemaphoreType.DMA
    return pl.pallas_call(
        exchange_kernel,
        out_shape=(
            jax.ShapeDtypeStruct((COLS, GA, 128), jnp.bfloat16),
            jax.ShapeDtypeStruct((ROWS, 2, COLS, 16, SW), jnp.bfloat16),
        ),
        in_specs=[vm, vm, vm],
        out_specs=(anywhere, anywhere),
        scratch_shapes=[
            pltpu.VMEM((SUB, ROWS, 16, SW), jnp.bfloat16),
            pltpu.VMEM((SUB, ROWS, 16, SW), jnp.bfloat16),
            pltpu.VMEM((GA, 128), jnp.bfloat16),
            dma((SUB, ROWS)), dma((SUB, ROWS)),
            dma((SUB, ROWS)), dma((2, COLS)),
            dma((SUB, 2, 20)), dma((SUB, 2, 20)),
            dma((2, 9)), dma((2, 9)),
            dma((SUB,)), dma((2,)), dma((SUB,)),
        ],
        compiler_params=pltpu.CompilerParams(
            collective_id=0, has_side_effects=True, vmem_limit_bytes=32 << 20
        ),
        name="exchange",
    )(xt, index.reshape(ROWS * SUB, SW), jnp.asarray(dft_tables()[3]))


TM = 256


def response_kernel(a_ref, b_ref, o_ref, rhs):
    @pl.when(pl.program_id(0) == 0)
    def _():
        def build(n, _):
            i, j = n // COLS, lax.rem(n, COLS)
            block = jnp.concatenate([b_ref[i, f, j] for f in range(2)], axis=1).astype(jnp.float32)
            re, im = block[:8], block[8:]
            rows = pl.ds(pl.multiple_of(j * 128 + i * 16, 16), 16)
            rhs[rows, :GB] = (-block).astype(jnp.bfloat16)
            rhs[rows, GB:] = jnp.concatenate([-im, re], axis=0).astype(jnp.bfloat16)
            return 0

        lax.fori_loop(0, ROWS * COLS, build, 0)

    lhs = jnp.concatenate([a_ref[j] for j in range(COLS)], axis=1)
    for q in range(2):
        o_ref[q] = jnp.dot(lhs, rhs[:, q * GB : (q + 1) * GB], preferred_element_type=jnp.float32)


def contract(a, b):
    return pl.pallas_call(
        response_kernel,
        out_shape=jax.ShapeDtypeStruct((2, GA, GB), jnp.float32),
        grid=(GA // TM,),
        in_specs=[
            pl.BlockSpec((COLS, TM, 128), lambda m: (0, m, 0)),
            pl.BlockSpec((ROWS, 2, COLS, 16, SW), lambda m: (0, 0, 0, 0, 0), pipeline_mode=pl.Buffered(1)),
        ],
        out_specs=pl.BlockSpec((2, TM, GB), lambda m: (0, m, 0)),
        scratch_shapes=[pltpu.VMEM((COLS * 128, 2 * GB), jnp.bfloat16)],
        compiler_params=pltpu.CompilerParams(vmem_limit_bytes=48 << 20),
        name="contract",
    )(a, b)


def body(valence, conduction, valence_energy, conduction_energy, band_pairs, grid_index):
    xt = spectrum(valence, conduction, valence_energy, conduction_energy, band_pairs)
    a, b = exchange(xt, grid_index)
    return contract(a, b)


def solution(mesh):
    return jax.shard_map(
        body,
        mesh=mesh,
        in_specs=(P(), P(), P(), P(), P(("row", "col"), None), P()),
        out_specs=P(None, "row", "col"),
        check_vma=False,
    )
```

```python
import math
import numpy as np
import jax
import jax.numpy as jnp
import ml_dtypes
from jax import lax
from jax.sharding import PartitionSpec as P
from jax.experimental import pallas as pl
from jax.experimental.pallas import tpu as pltpu

N1 = N2 = N3 = 32
KA, KB = 256, 128
NGV = 16384
NR = 32768
GW = 1024


def split_np(t):
    hi = t.astype(ml_dtypes.bfloat16)
    lo = (t - hi.astype(np.float64)).astype(ml_dtypes.bfloat16)
    return hi, lo


def dft_tables():
    a = np.arange(KA)
    r1, r2a = a // 8, a % 8
    ph = (np.outer(r1, r1) / 32.0 + np.outer(r2a, r2a) / 8.0) % 1.0
    c, s = np.cos(2 * np.pi * ph), np.sin(2 * np.pi * ph)
    ta = np.block([[c, s], [-s, c]])
    b = np.arange(KB)
    r2b, r3 = b // 32, b % 32
    ph = (np.outer(r2b, r2b) / 4.0 + np.outer(r3, r3) / 32.0) % 1.0
    c, s = np.cos(2 * np.pi * ph), np.sin(2 * np.pi * ph)
    tb = np.block([[c, s], [-s, c]])
    ph = np.outer(r2a, r2b) / 32.0
    tw = np.stack([np.cos(2 * np.pi * ph), np.sin(2 * np.pi * ph)]).astype(np.float32)
    ta_hi, ta_lo = split_np(ta)
    tb_hi, tb_lo = split_np(tb)
    fold = np.zeros((16, 128), ml_dtypes.bfloat16)
    for p in range(8):
        for ri in range(2):
            fold[ri * 8 + p, p * 16 + ri * 8 : p * 16 + ri * 8 + 8] = 1
    return np.stack([ta_hi, ta_lo]), np.stack([tb_hi, tb_lo]), tw, fold


def split(x):
    hi = x.astype(jnp.bfloat16)
    return hi, (x - hi.astype(jnp.float32)).astype(jnp.bfloat16)


def dot_f32(a, b, dims):
    return lax.dot_general(a, b, (dims, ((), ())), preferred_element_type=jnp.float32)


def spectrum_kernel(
    bands, v_energy, c_energy, valence, conduction, ta_hbm, tb_hbm, tw_hbm, xt,
    v_half, c_half, v_full, c_full, ta, tb, tw, sems,
):
    tables = [
        pltpu.make_async_copy(src, dst, sems.at[k])
        for k, (src, dst) in enumerate(((valence, v_half), (ta_hbm, ta), (tb_hbm, tb), (tw_hbm, tw)))
    ]

    def strip(p):
        rows = pl.ds(pl.multiple_of(bands[p, 1] // 8 * 8, 8), 8)
        return pltpu.make_async_copy(conduction.at[:, rows, :], c_half.at[p], sems.at[4 + p])

    tables[0].start()
    strip(0).start()
    strip(1).start()
    for copy in tables[1:]:
        copy.start()
    for p in range(2, 8):
        strip(p).start()

    tables[0].wait()

    def widen_v(a, _):
        lanes = pl.ds(pl.multiple_of(a * 128, 128), 128)
        rows = pl.ds(pl.multiple_of(a * 16, 16), 16)
        for q in range(2):
            v_full[q, rows, :] = v_half[q, :, lanes].astype(jnp.float32)
        return 0

    lax.fori_loop(0, KA, widen_v, 0, unroll=8)

    nn = ((1,), (0,))
    nt = ((1,), (1,))
    for h in range(4):
        for e in range(2):
            strip(2 * h + e).wait()

        def widen_c(a, _):
            lanes = pl.ds(pl.multiple_of(a * 128, 128), 128)
            rows = pl.ds(pl.multiple_of(a * 8, 8), 8)
            for e in range(2):
                for q in range(2):
                    c_full[h % 2, e, q, rows, :] = c_half[2 * h + e, q, :, lanes].astype(jnp.float32)
            return 0

        lax.fori_loop(0, KA, widen_c, 0, unroll=8)
        real, imag = [], []
        for e in range(2):
            p = 2 * h + e
            vr, vi = (v_full[q, pl.ds(bands[p, 0], KA, stride=16), :] for q in range(2))
            cr, ci = (c_full[h % 2, e, q, pl.ds(bands[p, 1] % 8, KA, stride=8), :] for q in range(2))
            real.append(vr * cr + vi * ci)
            imag.append(vr * ci - vi * cr)
        x = jnp.concatenate([jnp.concatenate(real, axis=1), jnp.concatenate(imag, axis=1)], axis=0)
        if h == 0:
            for copy in tables[1:]:
                copy.wait()
        xh, xl = split(x)
        z = dot_f32(ta[0], xh, nn) + (dot_f32(ta[0], xl, nn) + dot_f32(ta[1], xh, nn))
        for e in range(2):
            p = 2 * h + e
            zr, zi = z[:KA, e * KB : (e + 1) * KB], z[KA:, e * KB : (e + 1) * KB]
            t = jnp.concatenate([zr * tw[0] + zi * tw[1], zi * tw[0] - zr * tw[1]], axis=1)
            th, tl = split(t)
            s = dot_f32(tb[0], th, nt) + (dot_f32(tb[0], tl, nt) + dot_f32(tb[1], th, nt))
            gap = jnp.full((1, KA), v_energy[bands[p, 0]] - c_energy[bands[p, 1]], jnp.float32)
            scale = jnp.sqrt(-2.0 / (math.sqrt(1024) * gap)) * (1.0 / math.sqrt(N1 * N2 * N3))
            xt[p] = (s * scale).astype(jnp.bfloat16)


def spectrum(valence, conduction, valence_energy, conduction_energy, band_pairs):
    ta, tb, tw, _ = dft_tables()
    anywhere = pl.BlockSpec(memory_space=pltpu.HBM)
    scalars = pl.BlockSpec(memory_space=pltpu.SMEM)
    bf, f32 = jnp.bfloat16, jnp.float32
    return pl.pallas_call(
        spectrum_kernel,
        out_shape=jax.ShapeDtypeStruct((8, 256, 256), bf),
        in_specs=[scalars] * 3 + [anywhere] * 5,
        out_specs=pl.BlockSpec(memory_space=pltpu.VMEM),
        scratch_shapes=[
            pltpu.VMEM((2, 16, NR), bf),
            pltpu.VMEM((8, 2, 8, NR), bf),
            pltpu.VMEM((2, KA * 16, 128), f32),
            pltpu.VMEM((2, 2, 2, KA * 8, 128), f32),
            pltpu.VMEM(ta.shape, bf),
            pltpu.VMEM(tb.shape, bf),
            pltpu.VMEM(tw.shape, f32),
            pltpu.SemaphoreType.DMA((12,)),
        ],
        compiler_params=pltpu.CompilerParams(vmem_limit_bytes=48 << 20),
        name="spectrum",
    )(band_pairs, valence_energy, conduction_energy, valence, conduction,
      jnp.asarray(ta), jnp.asarray(tb), jnp.asarray(tw))


MESH = pl.DeviceIdType.MESH
ROWS, COLS = 8, 16
GA, GB = NGV // ROWS, NGV // COLS
SUB, SW = 4, 512
HALF, PART = SW // 2, SW // 4
SIDES = ((0, 1), (1, 3))
SLOTS = (0, 3, 1, 2)


def exchange_kernel(
    xt, index_ref, fold_ref, a_ref, b_ref, ys, pa, at,
    a0s, a0r, b0s, b0t, b0r, a1s, a1r, a1f, b1s, b1r, b1f, own_t,
):
    row, col = lax.axis_index("row"), lax.axis_index("col")
    x, core = row // 2, row % 2
    ty, tz, tx = ([(v + d) % 4 for d in range(4)] for v in (col // 4, col % 4, x))
    cell = [[ty[u] * 4 + tz[d] for d in range(4)] for u in range(4)]
    line = [tx[d] * 2 + core for d in range(4)]
    other = [tx[d] * 2 + 1 - core for d in range(4)]
    to_row = [(row + d) % ROWS for d in range(ROWS)]
    to_pair = [(col // 2 + d) % 8 for d in range(8)]
    odd = col % 2
    me = (row, col)

    def remote(src, dst, send, recv, device):
        return pltpu.make_async_remote_copy(
            src_ref=src, dst_ref=dst, send_sem=send, recv_sem=recv,
            device_id=device, device_id_type=MESH,
        )

    barrier = pltpu.get_barrier_semaphore()
    for d in range(1, ROWS):
        pl.semaphore_signal(barrier, inc=1, device_id=(to_row[d], col), device_id_type=MESH)
    for d in range(1, COLS):
        pl.semaphore_signal(barrier, inc=1, device_id=(row, (col + d) % COLS), device_id_type=MESH)


    def select(s, m):
        k = jnp.concatenate([index_ref[pl.ds((2 * m + e) * SUB + s, 1), :] for e in range(2)], axis=1)
        ka = (k >> 10) * 8 + ((k >> 5) & 7)
        kb = ((k >> 8) & 3) * 32 + (k & 31)
        hot = jnp.where(lax.broadcasted_iota(jnp.int32, (KA, GW), 0) == ka, 1.0, 0.0).astype(jnp.bfloat16)
        kb_hi = jnp.broadcast_to(kb >> 3, (8, GW))
        low = lax.broadcasted_iota(jnp.int32, (8, GW), 0) == (kb & 7)
        parts = []
        for p in range(8):
            r = jnp.dot(xt[p], hot, preferred_element_type=jnp.float32)
            for q in range(2):
                acc = r[q * KB : q * KB + 8]
                for j in range(1, 16):
                    acc = jnp.where(kb_hi == j, r[q * KB + j * 8 : q * KB + j * 8 + 8], acc)
                parts.append(jnp.where(low, acc, 0.0))
        part = jnp.concatenate(parts, axis=0).astype(jnp.bfloat16)
        y = jnp.dot(fold_ref[...], part, preferred_element_type=jnp.float32).astype(jnp.bfloat16)
        for e in range(2):
            ys[s, 2 * m + e] = y[:, e * SW : (e + 1) * SW]


    def b0(s, d, sem):
        i = to_pair[d]
        return remote(ys.at[s, i], b_ref.at[row, s % 2, col], sem, b0r.at[s % 2], (row, 2 * i + s // 2))

    def hand_out(s):
        if s == 0:
            pl.semaphore_wait(barrier, ROWS + COLS - 2)
        for d in range(1, ROWS):
            i = to_row[d]
            remote(ys.at[s, i], pa.at[s, row], a0s.at[s], a0r.at[s], (i, col)).start()
        pltpu.make_async_copy(ys.at[s, row], pa.at[s, row], a0r.at[s]).start()
        for d in range(1, 8):
            b0(s, d, b0s.at[s]).start()

        @pl.when(odd == s // 2)
        def _():
            pltpu.make_async_copy(ys.at[s, to_pair[0]], b_ref.at[row, s % 2, col], b0r.at[s % 2]).start()

        @pl.when(odd != s // 2)
        def _():
            b0(s, 0, b0t.at[s]).start()


    def along(h, first, d):
        return (row, cell[d][0] if (h == 0) == first else cell[0][d])

    def spot(h, u, d):
        return cell[u][d] if h == 0 else cell[d][u]

    def rows(s, h, part=None):
        if part is None:
            return pl.ds(s * SW + h * HALF, HALF)
        return pl.ds(s * SW + h * HALF + part * PART, PART)

    def a1(s, h, k, j, device, part=None, src=None):
        dst = a_ref.at[j, rows(s, h, part)]
        recv = a1f.at[s] if k is None else a1r.at[s, h, k]
        return remote(dst if src is None else src, dst, a1s.at[s], recv, device)

    def second(s, h, slot):
        u = SLOTS[slot]
        src = at.at[rows(s, h)] if u == 0 else None
        for n, d in SIDES:
            a1(s, h, 4 + slot * 2 + n, spot(h, u, 0), along(h, False, d), src=src).start()

    def keep_t(s):
        span = pl.ds(s * SW, SW)
        return pltpu.make_async_copy(at.at[span], a_ref.at[col, span], own_t.at[s])

    def turn(s):
        remote(pa.at[s], pa.at[s], a0s.at[s], a0r.at[s], me).wait_recv()
        for n in range(SW // 128):
            block = pa[s, :, :, n * 128 : (n + 1) * 128].reshape(128, 128)
            at[s * SW + n * 128 : s * SW + (n + 1) * 128, :] = block.astype(jnp.float32).T.astype(jnp.bfloat16)
        for h in range(2):
            for n, d in SIDES:
                a1(s, h, n, col, along(h, True, d), src=at.at[rows(s, h)]).start()
        for h in range(2):
            second(s, h, 0)
        keep_t(s).start()

    def near(s):
        for n, d in SIDES:
            for h in range(2):
                j = spot(h, 4 - d, 0)
                a1(s, h, n, j, me).wait_recv()
                a1(s, h, 2 + n, j, along(h, True, d), part=n).start()
                second(s, h, 1 + n)

    def far(s):
        for h in range(2):
            for n in range(2):
                a1(s, h, 2 + n, spot(h, 2, 0), me, part=n).wait_recv()
            second(s, h, 3)

    def pass_on(s, slot):
        u = SLOTS[slot]
        for n, d in SIDES:
            for h in range(2):
                j = spot(h, u, 4 - d)
                a1(s, h, 4 + slot * 2 + n, j, me).wait_recv()
                a1(s, h, None, j, along(h, False, d), part=n).start()


    def b1(f, k, i, device, part=None):
        ref = b_ref.at[i, f] if part is None else b_ref.at[i, f, pl.ds(part * 8, 8)]
        return remote(ref, ref, b1s.at[f], b1f.at[f] if k is None else b1r.at[f, k], device)

    def sides(f):
        ref = b_ref.at[row, f]
        remote(ref, ref, b1s.at[f], b0r.at[f], me).wait_recv()
        for n, d in SIDES:
            b1(f, n, row, (line[d], col)).start()
        b1(f, None, row, (other[0], col)).start()

    def sides_near(f):
        for n, d in SIDES:
            i = line[4 - d]
            b1(f, n, i, me).wait_recv()
            b1(f, 2 + n, i, (line[d], col), part=n).start()
            b1(f, None, i, (other[0], col)).start()

    def sides_far(f):
        for n in range(2):
            b1(f, 2 + n, line[2], me, part=n).wait_recv()
            b1(f, None, line[2], (other[0], col), part=n).start()


    events = []
    for s in range(SUB):
        events.append((4 * s + 3.9, lambda s=s: hand_out(s)))
        events.append((4 * s + TURN, lambda s=s: turn(s)))
        events.append((4 * s + NEAR, lambda s=s: near(s)))
        events.append((4 * s + FAR, lambda s=s: far(s)))
        for slot in range(4):
            events.append((PASS + PACE * s + 1.5 * slot, lambda s=s, slot=slot: pass_on(s, slot)))
        for delay, run in ((7.1, sides), (12.1, sides_near), (16.1, sides_far)):
            def guarded(s=s, run=run):
                @pl.when(odd == s // 2)
                def _():
                    run(s % 2)

            events.append((4 * s + delay, guarded))
    events.sort(key=lambda e: e[0])

    def step(n, _):
        for e in range(2):
            select(n // 2, (n % 2) * 2 + e)
        for k in range(8):
            now = [run for time, run in events if 2 * k <= time - 1.5 < 2 * k + 2]
            if now:
                @pl.when(n == k)
                def _(now=now):
                    for run in now:
                        run()
        return 0

    lax.fori_loop(0, 8, step, 0)
    for time, run in events:
        if time - 1.5 >= 16:
            run()


    for s in range(SUB):
        whole = a_ref.at[0]
        remote(whole, whole, a1s.at[s], a1f.at[s], me).wait_recv()
    for f in range(2):
        span = b_ref.at[pl.ds(0, 4), f]
        remote(span, span, b1s.at[f], b1f.at[f], me).wait_recv()
    for s in range(SUB):
        keep_t(s).wait()
        span = ys.at[s, pl.ds(0, 7)]
        remote(span, span, a0s.at[s], a0r.at[s], me).wait_send()
        remote(span, span, b0s.at[s], a0r.at[s], me).wait_send()

        @pl.when(odd != s // 2)
        def _():
            b0(s, 0, b0t.at[s]).wait_send()

        span = a_ref.at[pl.ds(0, 15), pl.ds(0, SW)]
        remote(span, span, a1s.at[s], a1f.at[s], me).wait_send()
    for f in range(2):
        span = b_ref.at[pl.ds(0, 7), f]
        remote(span, span, b1s.at[f], b1f.at[f], me).wait_send()


TURN, NEAR, FAR, PASS, PACE = 6, 8, 10, 10, 6


def exchange(xt, index):
    hbm, vm = pl.BlockSpec(memory_space=pltpu.HBM), pl.BlockSpec(memory_space=pltpu.VMEM)
    dma = pltpu.SemaphoreType.DMA
    return pl.pallas_call(
        exchange_kernel,
        out_shape=(
            jax.ShapeDtypeStruct((COLS, GA, 128), jnp.bfloat16),
            jax.ShapeDtypeStruct((ROWS, 2, COLS, 16, SW), jnp.bfloat16),
        ),
        in_specs=[vm, vm, vm],
        out_specs=(hbm, hbm),
        scratch_shapes=[
            pltpu.VMEM((SUB, ROWS, 16, SW), jnp.bfloat16),
            pltpu.VMEM((SUB, ROWS, 16, SW), jnp.bfloat16),
            pltpu.VMEM((GA, 128), jnp.bfloat16),
            dma((SUB,)), dma((SUB,)),
            dma((SUB,)), dma((SUB,)), dma((2,)),
            dma((SUB,)), dma((SUB, 2, 12)), dma((SUB,)),
            dma((2,)), dma((2, 4)), dma((2,)),
            dma((SUB,)),
        ],
        compiler_params=pltpu.CompilerParams(
            collective_id=0, has_side_effects=True, vmem_limit_bytes=32 << 20
        ),
        name="exchange",
    )(xt, index.reshape(ROWS * SUB, SW), jnp.asarray(dft_tables()[3]))


TM = 256


def response_kernel(a_ref, b_ref, o_ref, rhs):
    @pl.when(pl.program_id(0) == 0)
    def _():
        def build(n, _):
            i, j = n // COLS, lax.rem(n, COLS)
            block = jnp.concatenate([b_ref[i, f, j] for f in range(2)], axis=1).astype(jnp.float32)
            re, im = block[:8], block[8:]
            rows = pl.ds(pl.multiple_of(j * 128 + i * 16, 16), 16)
            rhs[rows, :GB] = (-block).astype(jnp.bfloat16)
            rhs[rows, GB:] = jnp.concatenate([-im, re], axis=0).astype(jnp.bfloat16)
            return 0

        lax.fori_loop(0, ROWS * COLS, build, 0)

    lhs = jnp.concatenate([a_ref[j] for j in range(COLS)], axis=1)
    for q in range(2):
        o_ref[q] = jnp.dot(lhs, rhs[:, q * GB : (q + 1) * GB], preferred_element_type=jnp.float32)


def contract(a, b):
    return pl.pallas_call(
        response_kernel,
        out_shape=jax.ShapeDtypeStruct((2, GA, GB), jnp.float32),
        grid=(GA // TM,),
        in_specs=[
            pl.BlockSpec((COLS, TM, 128), lambda m: (0, m, 0)),
            pl.BlockSpec((ROWS, 2, COLS, 16, SW), lambda m: (0, 0, 0, 0, 0), pipeline_mode=pl.Buffered(1)),
        ],
        out_specs=pl.BlockSpec((2, TM, GB), lambda m: (0, m, 0)),
        scratch_shapes=[pltpu.VMEM((COLS * 128, 2 * GB), jnp.bfloat16)],
        compiler_params=pltpu.CompilerParams(vmem_limit_bytes=48 << 20),
        name="contract",
    )(a, b)


def body(valence, conduction, valence_energy, conduction_energy, band_pairs, grid_index):
    xt = spectrum(valence, conduction, valence_energy, conduction_energy, band_pairs)
    a, b = exchange(xt, grid_index)
    return contract(a, b)


def solution(mesh):
    return jax.shard_map(
        body,
        mesh=mesh,
        in_specs=(P(), P(), P(), P(), P(("row", "col"), None), P()),
        out_specs=P(None, "row", "col"),
        check_vma=False,
    )
```

```python
import math
import numpy as np
import jax
import jax.numpy as jnp
import ml_dtypes
from jax import lax
from jax.sharding import PartitionSpec as P
from jax.experimental import pallas as pl
from jax.experimental.pallas import tpu as pltpu

N1 = N2 = N3 = 32
KA, KB = 256, 128
NGV = 16384
NR = 32768
GW = 1024


def split_np(t):
    hi = t.astype(ml_dtypes.bfloat16)
    lo = (t - hi.astype(np.float64)).astype(ml_dtypes.bfloat16)
    return hi, lo


def dft_tables():
    a = np.arange(KA)
    r1, r2a = a // 8, a % 8
    ph = (np.outer(r1, r1) / 32.0 + np.outer(r2a, r2a) / 8.0) % 1.0
    c, s = np.cos(2 * np.pi * ph), np.sin(2 * np.pi * ph)
    ta = np.block([[c, s], [-s, c]])
    b = np.arange(KB)
    r2b, r3 = b // 32, b % 32
    ph = (np.outer(r2b, r2b) / 4.0 + np.outer(r3, r3) / 32.0) % 1.0
    c, s = np.cos(2 * np.pi * ph), np.sin(2 * np.pi * ph)
    tb = np.block([[c, s], [-s, c]])
    ph = np.outer(r2a, r2b) / 32.0
    tw = np.stack([np.cos(2 * np.pi * ph), np.sin(2 * np.pi * ph)]).astype(np.float32)
    ta_hi, ta_lo = split_np(ta)
    tb_hi, tb_lo = split_np(tb)
    fold = np.zeros((16, 128), ml_dtypes.bfloat16)
    for p in range(8):
        for ri in range(2):
            fold[ri * 8 + p, p * 16 + ri * 8 : p * 16 + ri * 8 + 8] = 1
    return np.stack([ta_hi, ta_lo]), np.stack([tb_hi, tb_lo]), tw, fold


def split(x):
    hi = x.astype(jnp.bfloat16)
    return hi, (x - hi.astype(jnp.float32)).astype(jnp.bfloat16)


def dot_f32(a, b, dims):
    return lax.dot_general(a, b, (dims, ((), ())), preferred_element_type=jnp.float32)


def spectrum_kernel(
    bands, v_hbm, c_hbm, valence, conduction, ta_hbm, tb_hbm, tw_hbm, xt,
    v_energy, c_energy, v_half, c_half, v_full, c_full, ta, tb, tw, sems,
):
    tables = [
        pltpu.make_async_copy(src, dst, sems.at[k])
        for k, (src, dst) in enumerate(
            ((valence, v_half), (ta_hbm, ta), (tb_hbm, tb), (tw_hbm, tw), (v_hbm, v_energy), (c_hbm, c_energy))
        )
    ]

    def strip(p):
        rows = pl.ds(pl.multiple_of(bands[1, p] // 8 * 8, 8), 8)
        return pltpu.make_async_copy(conduction.at[:, rows, :], c_half.at[p], sems.at[6 + p])

    tables[0].start()
    strip(0).start()
    strip(1).start()
    for copy in tables[1:]:
        copy.start()
    for p in range(2, 8):
        strip(p).start()

    tables[0].wait()

    def widen_v(a, _):
        lanes = pl.ds(pl.multiple_of(a * 128, 128), 128)
        rows = pl.ds(pl.multiple_of(a * 16, 16), 16)
        for q in range(2):
            v_full[q, rows, :] = v_half[q, :, lanes].astype(jnp.float32)
        return 0

    lax.fori_loop(0, KA, widen_v, 0, unroll=8)

    nn = ((1,), (0,))
    nt = ((1,), (1,))
    for h in range(4):
        for e in range(2):
            strip(2 * h + e).wait()

        def widen_c(a, _):
            lanes = pl.ds(pl.multiple_of(a * 128, 128), 128)
            rows = pl.ds(pl.multiple_of(a * 8, 8), 8)
            for e in range(2):
                for q in range(2):
                    c_full[h % 2, e, q, rows, :] = c_half[2 * h + e, q, :, lanes].astype(jnp.float32)
            return 0

        lax.fori_loop(0, KA, widen_c, 0, unroll=8)
        real, imag = [], []
        for e in range(2):
            p = 2 * h + e
            vr, vi = (v_full[q, pl.ds(bands[0, p], KA, stride=16), :] for q in range(2))
            cr, ci = (c_full[h % 2, e, q, pl.ds(bands[1, p] % 8, KA, stride=8), :] for q in range(2))
            real.append(vr * cr + vi * ci)
            imag.append(vr * ci - vi * cr)
        x = jnp.concatenate([jnp.concatenate(real, axis=1), jnp.concatenate(imag, axis=1)], axis=0)
        if h == 0:
            for copy in tables[1:]:
                copy.wait()
        xh, xl = split(x)
        z = dot_f32(ta[0], xh, nn) + (dot_f32(ta[0], xl, nn) + dot_f32(ta[1], xh, nn))
        for e in range(2):
            p = 2 * h + e
            zr, zi = z[:KA, e * KB : (e + 1) * KB], z[KA:, e * KB : (e + 1) * KB]
            t = jnp.concatenate([zr * tw[0] + zi * tw[1], zi * tw[0] - zr * tw[1]], axis=1)
            th, tl = split(t)
            s = dot_f32(tb[0], th, nt) + (dot_f32(tb[0], tl, nt) + dot_f32(tb[1], th, nt))
            gap = jnp.full((1, KA), v_energy[bands[0, p]] - c_energy[bands[1, p]], jnp.float32)
            scale = jnp.sqrt(-2.0 / (math.sqrt(1024) * gap)) * (1.0 / math.sqrt(N1 * N2 * N3))
            xt[p] = (s * scale).astype(jnp.bfloat16)


def spectrum(valence, conduction, valence_energy, conduction_energy, band_pairs):
    ta, tb, tw, _ = dft_tables()
    anywhere = pl.BlockSpec(memory_space=pltpu.HBM)
    scalars = pl.BlockSpec(memory_space=pltpu.SMEM)
    bf, f32 = jnp.bfloat16, jnp.float32
    return pl.pallas_call(
        spectrum_kernel,
        out_shape=jax.ShapeDtypeStruct((8, 256, 256), bf),
        in_specs=[scalars] + [anywhere] * 7,
        out_specs=pl.BlockSpec(memory_space=pltpu.VMEM),
        scratch_shapes=[
            pltpu.SMEM(valence_energy.shape, f32),
            pltpu.SMEM(conduction_energy.shape, f32),
            pltpu.VMEM((2, 16, NR), bf),
            pltpu.VMEM((8, 2, 8, NR), bf),
            pltpu.VMEM((2, KA * 16, 128), f32),
            pltpu.VMEM((2, 2, 2, KA * 8, 128), f32),
            pltpu.VMEM(ta.shape, bf),
            pltpu.VMEM(tb.shape, bf),
            pltpu.VMEM(tw.shape, f32),
            pltpu.SemaphoreType.DMA((14,)),
        ],
        compiler_params=pltpu.CompilerParams(vmem_limit_bytes=48 << 20),
        name="spectrum",
    )(band_pairs.T,
      *(pltpu.with_memory_space_constraint(t, pltpu.HBM)
        for t in (valence_energy, conduction_energy, valence, conduction, jnp.asarray(ta), jnp.asarray(tb), jnp.asarray(tw))))


MESH = pl.DeviceIdType.MESH
ROWS, COLS = 8, 16
GA, GB = NGV // ROWS, NGV // COLS
SUB, SW = 4, 512
HALF, PART = SW // 2, SW // 4
SIDES = ((0, 1), (1, 3))
SLOTS = (0, 3, 1, 2)


def exchange_kernel(
    xt, index_ref, fold_ref, a_ref, rhs, part_ref, b_ref, ys, pa, at,
    a0s, a0r, b0s, b0t, b0r, a1s, a1r, a1f, b1s, b1r, b1f, own_t,
):
    row, col = lax.axis_index("row"), lax.axis_index("col")
    x, core = row // 2, row % 2
    ty, tz, tx = ([(v + d) % 4 for d in range(4)] for v in (col // 4, col % 4, x))
    cell = [[ty[u] * 4 + tz[d] for d in range(4)] for u in range(4)]
    line = [tx[d] * 2 + core for d in range(4)]
    other = [tx[d] * 2 + 1 - core for d in range(4)]
    to_row = [(row + d) % ROWS for d in range(ROWS)]
    to_pair = [(col // 2 + d) % 8 for d in range(8)]
    odd = col % 2
    me = (row, col)

    def remote(src, dst, send, recv, device):
        return pltpu.make_async_remote_copy(
            src_ref=src, dst_ref=dst, send_sem=send, recv_sem=recv,
            device_id=device, device_id_type=MESH,
        )

    barrier = pltpu.get_barrier_semaphore()
    for d in range(1, ROWS):
        pl.semaphore_signal(barrier, inc=1, device_id=(to_row[d], col), device_id_type=MESH)
    for d in range(1, COLS):
        pl.semaphore_signal(barrier, inc=1, device_id=(row, (col + d) % COLS), device_id_type=MESH)

    def place(s):
        return s % 2 * 2 + s // 2


    def select(s, m):
        k = jnp.concatenate([index_ref[pl.ds((2 * m + e) * SUB + place(s), 1), :] for e in range(2)], axis=1)
        ka = (k >> 10) * 8 + ((k >> 5) & 7)
        kb = ((k >> 8) & 3) * 32 + (k & 31)
        hot = jnp.where(lax.broadcasted_iota(jnp.int32, (KA, GW), 0) == ka, 1.0, 0.0).astype(jnp.bfloat16)
        kb_hi = jnp.broadcast_to(kb >> 3, (8, GW))
        low = lax.broadcasted_iota(jnp.int32, (8, GW), 0) == (kb & 7)
        parts = []
        for p in range(8):
            r = jnp.dot(xt[p], hot, preferred_element_type=jnp.float32)
            for q in range(2):
                acc = r[q * KB : q * KB + 8]
                for j in range(1, 16):
                    acc = jnp.where(kb_hi == j, r[q * KB + j * 8 : q * KB + j * 8 + 8], acc)
                parts.append(jnp.where(low, acc, 0.0))
        part = jnp.concatenate(parts, axis=0).astype(jnp.bfloat16)
        y = jnp.dot(fold_ref[...], part, preferred_element_type=jnp.float32).astype(jnp.bfloat16)
        for e in range(2):
            ys[s, 2 * m + e] = y[:, e * SW : (e + 1) * SW]


    def b0(s, d, sem):
        i = to_pair[d]
        return remote(ys.at[s, i], b_ref.at[row, s // 2, col], sem, b0r.at[s // 2], (row, 2 * i + s % 2))

    def hand_out(s):
        if s == 0:
            pl.semaphore_wait(barrier, ROWS + COLS - 2)
        for d in range(1, ROWS):
            i = to_row[d]
            remote(ys.at[s, i], pa.at[s, row], a0s.at[s], a0r.at[s], (i, col)).start()
        pltpu.make_async_copy(ys.at[s, row], pa.at[s, row], a0r.at[s]).start()
        for d in range(1, 8):
            b0(s, d, b0s.at[s]).start()

        @pl.when(odd == s % 2)
        def _():
            pltpu.make_async_copy(ys.at[s, to_pair[0]], b_ref.at[row, s // 2, col], b0r.at[s // 2]).start()

        @pl.when(odd != s % 2)
        def _():
            b0(s, 0, b0t.at[s]).start()


    def along(h, first, d):
        return (row, cell[d][0] if (h == 0) == first else cell[0][d])

    def spot(h, u, d):
        return cell[u][d] if h == 0 else cell[d][u]

    def rows(s, h, part=None):
        if part is None:
            return pl.ds(place(s) * SW + h * HALF, HALF)
        return pl.ds(place(s) * SW + h * HALF + part * PART, PART)

    def a1(s, h, k, j, device, part=None, src=None):
        dst = a_ref.at[j, rows(s, h, part)]
        recv = a1f.at[s] if k is None else a1r.at[s, h, k]
        return remote(dst if src is None else src, dst, a1s.at[s], recv, device)

    def second(s, h, slot):
        u = SLOTS[slot]
        src = at.at[rows(s, h)] if u == 0 else None
        for n, d in SIDES:
            a1(s, h, 4 + slot * 2 + n, spot(h, u, 0), along(h, False, d), src=src).start()

    def keep_t(s):
        span = pl.ds(place(s) * SW, SW)
        return pltpu.make_async_copy(at.at[span], a_ref.at[col, span], own_t.at[s])

    def turn(s):
        remote(pa.at[s], pa.at[s], a0s.at[s], a0r.at[s], me).wait_recv()
        for n in range(SW // 128):
            block = pa[s, :, :, n * 128 : (n + 1) * 128].reshape(128, 128)
            start = place(s) * SW + n * 128
            at[start : start + 128, :] = block.astype(jnp.float32).T.astype(jnp.bfloat16)
        for h in range(2):
            for n, d in SIDES:
                a1(s, h, n, col, along(h, True, d), src=at.at[rows(s, h)]).start()
        for h in range(2):
            second(s, h, 0)
        keep_t(s).start()

    def near(s):
        for n, d in SIDES:
            for h in range(2):
                j = spot(h, 4 - d, 0)
                a1(s, h, n, j, me).wait_recv()
                a1(s, h, 2 + n, j, along(h, True, d), part=n).start()
                second(s, h, 1 + n)

    def far(s):
        for h in range(2):
            for n in range(2):
                a1(s, h, 2 + n, spot(h, 2, 0), me, part=n).wait_recv()
            second(s, h, 3)

    def pass_on(s, slot):
        u = SLOTS[slot]
        for n, d in SIDES:
            for h in range(2):
                j = spot(h, u, 4 - d)
                a1(s, h, 4 + slot * 2 + n, j, me).wait_recv()
                a1(s, h, None, j, along(h, False, d), part=n).start()


    def b1(f, k, i, device, part=None):
        ref = b_ref.at[i, f] if part is None else b_ref.at[i, f, pl.ds(part * 8, 8)]
        return remote(ref, ref, b1s.at[f], b1f.at[f] if k is None else b1r.at[f, k], device)

    def sides(f):
        ref = b_ref.at[row, f]
        remote(ref, ref, b1s.at[f], b0r.at[f], me).wait_recv()
        for n, d in SIDES:
            b1(f, n, row, (line[d], col)).start()
        b1(f, None, row, (other[0], col)).start()

    def sides_near(f):
        for n, d in SIDES:
            i = line[4 - d]
            b1(f, n, i, me).wait_recv()
            b1(f, 2 + n, i, (line[d], col), part=n).start()
            b1(f, None, i, (other[0], col)).start()

    def sides_far(f):
        for n in range(2):
            b1(f, 2 + n, line[2], me, part=n).wait_recv()
            b1(f, None, line[2], (other[0], col), part=n).start()


    events = []
    for s in range(SUB):
        events.append((4 * s + 3.9, lambda s=s: hand_out(s)))
        events.append((4 * s + TURN, lambda s=s: turn(s)))
        events.append((4 * s + NEAR, lambda s=s: near(s)))
        events.append((4 * s + FAR, lambda s=s: far(s)))
        for slot in range(4):
            events.append((PASS + PACE * s + 1.5 * slot, lambda s=s, slot=slot: pass_on(s, slot)))
        for delay, run in ((7.1, sides), (11.6, sides_near), (15.4, sides_far)):
            def guarded(s=s, run=run):
                @pl.when(odd == s % 2)
                def _():
                    run(s // 2)

            events.append((4 * s + delay, guarded))
    events.sort(key=lambda e: e[0])

    def step(n, _):
        for e in range(2):
            select(n // 2, (n % 2) * 2 + e)
        for k in range(8):
            now = [run for time, run in events if 2 * k + 1.5 <= time < 2 * k + 3.5]
            if now:
                @pl.when(n == k)
                def _(now=now):
                    for run in now:
                        run()
        return 0

    lax.fori_loop(0, 8, step, 0)
    for time, run in events:
        if 17.5 <= time < UNITS[0]:
            run()


    def build(f):
        span = b_ref.at[pl.ds(0, 4), f]
        remote(span, span, b1s.at[f], b1f.at[f], me).wait_recv()

        def cross(n, _):
            i, j = n // COLS, n % COLS
            block = b_ref[i, f, j].astype(jnp.float32)
            span = pl.ds(pl.multiple_of(j * 128 + i * 16, 16), 16)
            rhs[f, span, :SW] = (-block).astype(jnp.bfloat16)
            rhs[f, span, SW:] = jnp.concatenate([-block[8:], block[:8]], axis=0).astype(jnp.bfloat16)
            return 0

        lax.fori_loop(0, ROWS * COLS, cross, 0, unroll=4)

    def complete(s):
        whole = a_ref.at[0]
        remote(whole, whole, a1s.at[s], a1f.at[s], me).wait_recv()
        keep_t(s).wait()

    ready = {0: [lambda: complete(0), lambda: build(0)], 1: [lambda: complete(1)], 2: [lambda: build(1)],
             4: [lambda: complete(2)]}

    def unit(t, _):
        for k, runs in ready.items():
            @pl.when(t == k)
            def _(runs=runs):
                for run in runs:
                    run()

        late = t // 4
        f = (1 - late) * (t // 2) + late * (t % 2)
        block = (1 - late) * (t % 2) * 2 + late
        for e in range(SW // TM):
            span = pl.ds(pl.multiple_of(block * SW + e * TM, TM), TM)
            lhs = jnp.concatenate([a_ref[j, span, :] for j in range(COLS)], axis=1)
            for q in range(2):
                part_ref[q, f, span, :] = jnp.dot(
                    lhs, rhs[f, :, q * SW : (q + 1) * SW], preferred_element_type=jnp.float32
                )
        for k in range(len(UNITS)):
            upper = UNITS[k + 1] if k + 1 < len(UNITS) else 1e9
            now = [run for time, run in events if UNITS[k] <= time < upper]
            if now:
                @pl.when(t == k)
                def _(now=now):
                    for run in now:
                        run()
        return 0

    lax.fori_loop(0, len(UNITS), unit, 0)


    for s in range(READY // SW, SUB):
        complete(s)
    for s in range(SUB):
        span = ys.at[s, pl.ds(0, 7)]
        remote(span, span, a0s.at[s], a0r.at[s], me).wait_send()
        remote(span, span, b0s.at[s], a0r.at[s], me).wait_send()

        @pl.when(odd != s % 2)
        def _():
            b0(s, 0, b0t.at[s]).wait_send()

        span = a_ref.at[pl.ds(0, 15), pl.ds(0, SW)]
        remote(span, span, a1s.at[s], a1f.at[s], me).wait_send()
    for f in range(2):
        span = b_ref.at[pl.ds(0, 7), f]
        remote(span, span, b1s.at[f], b1f.at[f], me).wait_send()


TURN, NEAR, FAR, PASS, PACE = 6, 8, 10, 10, 6
UNITS = (21, 24, 31.1, 33, 34, 35)
TM = 256
READY = 1536


def exchange(xt, index):
    vm = pl.BlockSpec(memory_space=pltpu.VMEM)
    dma = pltpu.SemaphoreType.DMA
    return pl.pallas_call(
        exchange_kernel,
        out_shape=(
            jax.ShapeDtypeStruct((COLS, GA, 128), jnp.bfloat16),
            jax.ShapeDtypeStruct((2, COLS * 128, GB), jnp.bfloat16),
            jax.ShapeDtypeStruct((2, 2, READY, SW), jnp.float32),
        ),
        in_specs=[vm, vm, vm],
        out_specs=(vm, vm, vm),
        scratch_shapes=[
            pltpu.VMEM((ROWS, 2, COLS, 16, SW), jnp.bfloat16),
            pltpu.VMEM((SUB, ROWS, 16, SW), jnp.bfloat16),
            pltpu.VMEM((SUB, ROWS, 16, SW), jnp.bfloat16),
            pltpu.VMEM((GA, 128), jnp.bfloat16),
            dma((SUB,)), dma((SUB,)),
            dma((SUB,)), dma((SUB,)), dma((2,)),
            dma((SUB,)), dma((SUB, 2, 12)), dma((SUB,)),
            dma((2,)), dma((2, 4)), dma((2,)),
            dma((SUB,)),
        ],
        compiler_params=pltpu.CompilerParams(
            collective_id=0, has_side_effects=True, vmem_limit_bytes=24 << 20
        ),
        name="exchange",
    )(xt, index.reshape(ROWS * SUB, SW), jnp.asarray(dft_tables()[3]))


TAIL = 128


def response_kernel(a_ref, rhs, part_ref, o_ref, stage, sems):
    copies = []

    def out(src, q, f, rows):
        copy = pltpu.make_async_copy(src, o_ref.at[q, rows, pl.ds(f * SW, SW)], sems.at[len(copies)])
        copy.start()
        copies.append(copy)

    for q in range(2):
        for f in range(2):
            out(part_ref.at[q, f], q, f, pl.ds(0, READY))
    for t in range((GA - READY) // TAIL):
        rows = pl.ds(READY + t * TAIL, TAIL)
        lhs = jnp.concatenate([a_ref[j, rows, :] for j in range(COLS)], axis=1)
        for f in range(2):
            for q in range(2):
                stage[t, q, f] = jnp.dot(
                    lhs, rhs[f, :, q * SW : (q + 1) * SW], preferred_element_type=jnp.float32
                )
                out(stage.at[t, q, f], q, f, rows)
    for copy in copies:
        copy.wait()


def contract(a, rhs, part):
    vm = pl.BlockSpec(memory_space=pltpu.VMEM)
    tiles = (GA - READY) // TAIL
    return pl.pallas_call(
        response_kernel,
        out_shape=jax.ShapeDtypeStruct((2, GA, GB), jnp.float32),
        in_specs=[vm, vm, vm],
        out_specs=pl.BlockSpec(memory_space=pltpu.HBM),
        scratch_shapes=[
            pltpu.VMEM((tiles, 2, 2, TAIL, SW), jnp.float32),
            pltpu.SemaphoreType.DMA((4 + 4 * tiles,)),
        ],
        compiler_params=pltpu.CompilerParams(vmem_limit_bytes=24 << 20),
        name="contract",
    )(a, rhs, part)


def body(valence, conduction, valence_energy, conduction_energy, band_pairs, grid_index):
    xt = spectrum(valence, conduction, valence_energy, conduction_energy, band_pairs)
    return contract(*exchange(xt, grid_index))


def solution(mesh):
    return jax.shard_map(
        body,
        mesh=mesh,
        in_specs=(P(), P(), P(), P(), P(("row", "col"), None), P()),
        out_specs=P(None, "row", "col"),
        check_vma=False,
    )
```

```python
import math
import numpy as np
import jax
import jax.numpy as jnp
import ml_dtypes
from jax import lax
from jax.sharding import PartitionSpec as P
from jax.experimental import pallas as pl
from jax.experimental.pallas import tpu as pltpu

N1 = N2 = N3 = 32
KA, KB = 256, 128
NGV = 16384
NR = 32768
GW = 2048


def split_np(t):
    hi = t.astype(ml_dtypes.bfloat16)
    lo = (t - hi.astype(np.float64)).astype(ml_dtypes.bfloat16)
    return hi, lo


def dft_tables():
    a = np.arange(KA)
    r1, r2a = a // 8, a % 8
    ph = (np.outer(r1, r1) / 32.0 + np.outer(r2a, r2a) / 8.0) % 1.0
    c, s = np.cos(2 * np.pi * ph), np.sin(2 * np.pi * ph)
    ta = np.block([[c, s], [-s, c]])
    b = np.arange(KB)
    r2b, r3 = b // 32, b % 32
    ph = (np.outer(r2b, r2b) / 4.0 + np.outer(r3, r3) / 32.0) % 1.0
    c, s = np.cos(2 * np.pi * ph), np.sin(2 * np.pi * ph)
    tb = np.block([[c, s], [-s, c]])
    ph = np.outer(r2a, r2b) / 32.0
    tw = np.stack([np.cos(2 * np.pi * ph), np.sin(2 * np.pi * ph)]).astype(np.float32)
    ta_hi, ta_lo = split_np(ta)
    tb_hi, tb_lo = split_np(tb)
    fold = np.zeros((16, 128), ml_dtypes.bfloat16)
    for p in range(8):
        for ri in range(2):
            fold[ri * 8 + p, p * 16 + ri * 8 : p * 16 + ri * 8 + 8] = 1
    return np.stack([ta_hi, ta_lo]), np.stack([tb_hi, tb_lo]), tw, fold


def split(x):
    hi = x.astype(jnp.bfloat16)
    return hi, (x - hi.astype(jnp.float32)).astype(jnp.bfloat16)


def dot_f32(a, b, dims):
    return lax.dot_general(a, b, (dims, ((), ())), preferred_element_type=jnp.float32)


def spectrum_kernel(
    bands, v_hbm, c_hbm, valence, conduction, ta_hbm, tb_hbm, tw_hbm, xt,
    v_energy, c_energy, v_half, c_half, v_full, c_full, ta, tb, tw, sems,
):
    tables = [
        pltpu.make_async_copy(src, dst, sems.at[k])
        for k, (src, dst) in enumerate(
            ((valence, v_half), (ta_hbm, ta), (tb_hbm, tb), (tw_hbm, tw), (v_hbm, v_energy), (c_hbm, c_energy))
        )
    ]

    def strip(p):
        rows = pl.ds(pl.multiple_of(bands[1, p] // 8 * 8, 8), 8)
        return pltpu.make_async_copy(conduction.at[:, rows, :], c_half.at[p], sems.at[6 + p])

    tables[0].start()
    strip(0).start()
    strip(1).start()
    for copy in tables[1:]:
        copy.start()
    for p in range(2, 8):
        strip(p).start()

    tables[0].wait()

    def widen_v(a, _):
        lanes = pl.ds(pl.multiple_of(a * 128, 128), 128)
        rows = pl.ds(pl.multiple_of(a * 16, 16), 16)
        for q in range(2):
            v_full[q, rows, :] = v_half[q, :, lanes].astype(jnp.float32)
        return 0

    lax.fori_loop(0, KA, widen_v, 0, unroll=8)

    nn = ((1,), (0,))
    nt = ((1,), (1,))

    def widen_c(h):
        for e in range(2):
            strip(2 * h + e).wait()
        for a in range(KA):
            for e in range(2):
                for q in range(2):
                    c_full[h % 2, e, q, a * 8 : a * 8 + 8, :] = c_half[
                        2 * h + e, q, :, a * 128 : a * 128 + 128
                    ].astype(jnp.float32)

    widen_c(0)
    for copy in tables[1:]:
        copy.wait()
    for h in range(4):
        real, imag = [], []
        for e in range(2):
            p = 2 * h + e
            vr, vi = (v_full[q, pl.ds(bands[0, p], KA, stride=16), :] for q in range(2))
            cr, ci = (c_full[h % 2, e, q, pl.ds(bands[1, p] % 8, KA, stride=8), :] for q in range(2))
            real.append(vr * cr + vi * ci)
            imag.append(vr * ci - vi * cr)
        x = jnp.concatenate([jnp.concatenate(real, axis=1), jnp.concatenate(imag, axis=1)], axis=0)
        xh, xl = split(x)
        z = dot_f32(
            jnp.concatenate([ta[0], ta[0], ta[1]], axis=1), jnp.concatenate([xh, xl, xh], axis=0), nn
        )
        if h < 3:
            widen_c(h + 1)
        for e in range(2):
            p = 2 * h + e
            zr, zi = z[:KA, e * KB : (e + 1) * KB], z[KA:, e * KB : (e + 1) * KB]
            t = jnp.concatenate([zr * tw[0] + zi * tw[1], zi * tw[0] - zr * tw[1]], axis=1)
            th, tl = split(t)
            s = dot_f32(
                jnp.concatenate([tb[0], tb[0], tb[1]], axis=1), jnp.concatenate([th, tl, th], axis=1), nt
            )
            gap = jnp.full((1, KA), v_energy[bands[0, p]] - c_energy[bands[1, p]], jnp.float32)
            scale = jnp.sqrt(-2.0 / (math.sqrt(1024) * gap)) * (1.0 / math.sqrt(N1 * N2 * N3))
            xt[p] = (s * scale).astype(jnp.bfloat16)


def spectrum(valence, conduction, valence_energy, conduction_energy, band_pairs):
    ta, tb, tw, _ = dft_tables()
    anywhere = pl.BlockSpec(memory_space=pltpu.HBM)
    scalars = pl.BlockSpec(memory_space=pltpu.SMEM)
    bf, f32 = jnp.bfloat16, jnp.float32
    return pl.pallas_call(
        spectrum_kernel,
        out_shape=jax.ShapeDtypeStruct((8, 256, 256), bf),
        in_specs=[scalars] + [anywhere] * 7,
        out_specs=pl.BlockSpec(memory_space=pltpu.VMEM),
        scratch_shapes=[
            pltpu.SMEM(valence_energy.shape, f32),
            pltpu.SMEM(conduction_energy.shape, f32),
            pltpu.VMEM((2, 16, NR), bf),
            pltpu.VMEM((8, 2, 8, NR), bf),
            pltpu.VMEM((2, KA * 16, 128), f32),
            pltpu.VMEM((2, 2, 2, KA * 8, 128), f32),
            pltpu.VMEM(ta.shape, bf),
            pltpu.VMEM(tb.shape, bf),
            pltpu.VMEM(tw.shape, f32),
            pltpu.SemaphoreType.DMA((14,)),
        ],
        compiler_params=pltpu.CompilerParams(vmem_limit_bytes=48 << 20),
        name="spectrum",
    )(band_pairs.T,
      *(pltpu.with_memory_space_constraint(t, pltpu.HBM)
        for t in (valence_energy, conduction_energy, valence, conduction, jnp.asarray(ta), jnp.asarray(tb), jnp.asarray(tw))))


MESH = pl.DeviceIdType.MESH
ROWS, COLS = 8, 16
GA, GB = NGV // ROWS, NGV // COLS
SUB, SW = 4, 512
HALF, PART = SW // 2, SW // 4
SIDES = ((0, 1), (1, 3))
SLOTS = (0, 3, 1, 2)


def exchange_kernel(
    xt, index_ref, fold_ref, a_ref, rhs, part_ref, b_ref, ys, pa, at,
    a0s, a0r, b0s, b0t, b0r, a1s, a1r, a1f, b1s, b1r, b1f, own_t,
):
    row, col = lax.axis_index("row"), lax.axis_index("col")
    x, core = row // 2, row % 2
    ty, tz, tx = ([(v + d) % 4 for d in range(4)] for v in (col // 4, col % 4, x))
    cell = [[ty[u] * 4 + tz[d] for d in range(4)] for u in range(4)]
    line = [tx[d] * 2 + core for d in range(4)]
    other = [tx[d] * 2 + 1 - core for d in range(4)]
    to_row = [(row + d) % ROWS for d in range(ROWS)]
    to_pair = [(col // 2 + d) % 8 for d in range(8)]
    odd = col % 2
    me = (row, col)

    def remote(src, dst, send, recv, device):
        return pltpu.make_async_remote_copy(
            src_ref=src, dst_ref=dst, send_sem=send, recv_sem=recv,
            device_id=device, device_id_type=MESH,
        )

    barrier = pltpu.get_barrier_semaphore()
    for d in range(1, ROWS):
        pl.semaphore_signal(barrier, inc=1, device_id=(to_row[d], col), device_id_type=MESH)
    for d in range(1, COLS):
        pl.semaphore_signal(barrier, inc=1, device_id=(row, (col + d) % COLS), device_id_type=MESH)

    def place(s):
        return s % 2 * 2 + s // 2


    def select(s, m):
        k = jnp.concatenate([index_ref[pl.ds((4 * m + e) * SUB + place(s), 1), :] for e in range(4)], axis=1)
        ka = (k >> 10) * 8 + ((k >> 5) & 7)
        kb = ((k >> 8) & 3) * 32 + (k & 31)
        hot = jnp.where(lax.broadcasted_iota(jnp.int32, (KA, GW), 0) == ka, 1.0, 0.0).astype(jnp.bfloat16)
        kb_hi = jnp.broadcast_to(kb >> 3, (8, GW))
        low = lax.broadcasted_iota(jnp.int32, (8, GW), 0) == (kb & 7)
        parts = []
        for p in range(8):
            r = jnp.dot(xt[p], hot, preferred_element_type=jnp.float32)
            for q in range(2):
                acc = r[q * KB : q * KB + 8]
                for j in range(1, 16):
                    acc = jnp.where(kb_hi == j, r[q * KB + j * 8 : q * KB + j * 8 + 8], acc)
                parts.append(jnp.where(low, acc, 0.0))
        part = jnp.concatenate(parts, axis=0).astype(jnp.bfloat16)
        y = jnp.dot(fold_ref[...], part, preferred_element_type=jnp.float32).astype(jnp.bfloat16)
        for e in range(4):
            ys[s, 4 * m + e] = y[:, e * SW : (e + 1) * SW]


    def b0(s, d, sem):
        i = to_pair[d]
        return remote(ys.at[s, i], b_ref.at[row, s // 2, col], sem, b0r.at[s // 2], (row, 2 * i + s % 2))

    def hand_out(s):
        if s == 0:
            pl.semaphore_wait(barrier, ROWS + COLS - 2)
        for d in range(1, ROWS):
            i = to_row[d]
            remote(ys.at[s, i], pa.at[s, row], a0s.at[s], a0r.at[s], (i, col)).start()
        pltpu.make_async_copy(ys.at[s, row], pa.at[s, row], a0r.at[s]).start()
        for d in range(1, 8):
            b0(s, d, b0s.at[s]).start()

        @pl.when(odd == s % 2)
        def _():
            pltpu.make_async_copy(ys.at[s, to_pair[0]], b_ref.at[row, s // 2, col], b0r.at[s // 2]).start()

        @pl.when(odd != s % 2)
        def _():
            b0(s, 0, b0t.at[s]).start()


    def along(h, first, d):
        return (row, cell[d][0] if (h == 0) == first else cell[0][d])

    def spot(h, u, d):
        return cell[u][d] if h == 0 else cell[d][u]

    def rows(s, h, part=None):
        if part is None:
            return pl.ds(place(s) * SW + h * HALF, HALF)
        return pl.ds(place(s) * SW + h * HALF + part * PART, PART)

    def a1(s, h, k, j, device, part=None, src=None):
        dst = a_ref.at[j, rows(s, h, part)]
        recv = a1f.at[s] if k is None else a1r.at[s, h, k]
        return remote(dst if src is None else src, dst, a1s.at[s], recv, device)

    def second(s, h, slot):
        u = SLOTS[slot]
        src = at.at[rows(s, h)] if u == 0 else None
        for n, d in SIDES:
            a1(s, h, 4 + slot * 2 + n, spot(h, u, 0), along(h, False, d), src=src).start()

    def keep_t(s):
        span = pl.ds(place(s) * SW, SW)
        return pltpu.make_async_copy(at.at[span], a_ref.at[col, span], own_t.at[s])

    def turn(s):
        remote(pa.at[s], pa.at[s], a0s.at[s], a0r.at[s], me).wait_recv()
        for n in range(SW // 128):
            block = pa[s, :, :, n * 128 : (n + 1) * 128].reshape(128, 128)
            start = place(s) * SW + n * 128
            at[start : start + 128, :] = block.astype(jnp.float32).T.astype(jnp.bfloat16)
        for h in range(2):
            for n, d in SIDES:
                a1(s, h, n, col, along(h, True, d), src=at.at[rows(s, h)]).start()
        for h in range(2):
            second(s, h, 0)
        keep_t(s).start()

    def near(s):
        for n, d in SIDES:
            for h in range(2):
                j = spot(h, 4 - d, 0)
                a1(s, h, n, j, me).wait_recv()
                a1(s, h, 2 + n, j, along(h, True, d), part=n).start()
                second(s, h, 1 + n)

    def far(s):
        for h in range(2):
            for n in range(2):
                a1(s, h, 2 + n, spot(h, 2, 0), me, part=n).wait_recv()
            second(s, h, 3)

    def pass_on(s, slot):
        u = SLOTS[slot]
        for n, d in SIDES:
            for h in range(2):
                j = spot(h, u, 4 - d)
                a1(s, h, 4 + slot * 2 + n, j, me).wait_recv()
                a1(s, h, None, j, along(h, False, d), part=n).start()


    def b1(f, k, i, device, part=None):
        ref = b_ref.at[i, f] if part is None else b_ref.at[i, f, pl.ds(part * 8, 8)]
        return remote(ref, ref, b1s.at[f], b1f.at[f] if k is None else b1r.at[f, k], device)

    def sides(f):
        ref = b_ref.at[row, f]
        remote(ref, ref, b1s.at[f], b0r.at[f], me).wait_recv()
        for n, d in SIDES:
            b1(f, n, row, (line[d], col)).start()
        b1(f, None, row, (other[0], col)).start()

    def sides_near(f):
        for n, d in SIDES:
            i = line[4 - d]
            b1(f, n, i, me).wait_recv()
            b1(f, 2 + n, i, (line[d], col), part=n).start()
            b1(f, None, i, (other[0], col)).start()

    def sides_far(f):
        for n in range(2):
            b1(f, 2 + n, line[2], me, part=n).wait_recv()
            b1(f, None, line[2], (other[0], col), part=n).start()


    events = []
    for s in range(SUB):
        events.append((4 * s + 3.9, lambda s=s: hand_out(s)))
        events.append((4 * s + TURN, lambda s=s: turn(s)))
        events.append((4 * s + NEAR, lambda s=s: near(s)))
        events.append((4 * s + FAR, lambda s=s: far(s)))
        for slot in range(4):
            events.append((PASS + PACE * s + 1.5 * slot, lambda s=s, slot=slot: pass_on(s, slot)))
        for delay, run in ((7.1, sides), (11.6, sides_near), (15.4, sides_far)):
            def guarded(s=s, run=run):
                @pl.when(odd == s % 2)
                def _():
                    run(s // 2)

            events.append((4 * s + delay, guarded))
    events.sort(key=lambda e: e[0])

    def step(n, _):
        select(n // 2, n % 2)
        for k in range(8):
            now = [run for time, run in events if 2 * k + 1.5 <= time < 2 * k + 3.5]
            if now:
                @pl.when(n == k)
                def _(now=now):
                    for run in now:
                        run()
        return 0

    lax.fori_loop(0, 8, step, 0)
    for time, run in events:
        if 17.5 <= time < UNITS[0]:
            run()


    def build(f):
        span = b_ref.at[pl.ds(0, 4), f]
        remote(span, span, b1s.at[f], b1f.at[f], me).wait_recv()

        def cross(n, _):
            i, j = n // COLS, n % COLS
            block = b_ref[i, f, j].astype(jnp.float32)
            span = pl.ds(pl.multiple_of(j * 128 + i * 16, 16), 16)
            rhs[f, span, :SW] = (-block).astype(jnp.bfloat16)
            rhs[f, span, SW:] = jnp.concatenate([-block[8:], block[:8]], axis=0).astype(jnp.bfloat16)
            return 0

        lax.fori_loop(0, ROWS * COLS, cross, 0, unroll=4)

    def complete(s):
        whole = a_ref.at[0]
        remote(whole, whole, a1s.at[s], a1f.at[s], me).wait_recv()
        keep_t(s).wait()

    ready = {0: [lambda: complete(0), lambda: build(0)], 1: [lambda: complete(1)], 2: [lambda: build(1)],
             4: [lambda: complete(2)]}

    def unit(t, _):
        for k, runs in ready.items():
            @pl.when(t == k)
            def _(runs=runs):
                for run in runs:
                    run()

        late = t // 4
        f = (1 - late) * (t // 2) + late * (t % 2)
        block = (1 - late) * (t % 2) * 2 + late
        for e in range(SW // TM):
            span = pl.ds(pl.multiple_of(block * SW + e * TM, TM), TM)
            lhs = jnp.concatenate([a_ref[j, span, :] for j in range(COLS)], axis=1)
            for q in range(2):
                part_ref[q, f, span, :] = jnp.dot(
                    lhs, rhs[f, :, q * SW : (q + 1) * SW], preferred_element_type=jnp.float32
                )
        for k in range(len(UNITS)):
            upper = UNITS[k + 1] if k + 1 < len(UNITS) else 1e9
            now = [run for time, run in events if UNITS[k] <= time < upper]
            if now:
                @pl.when(t == k)
                def _(now=now):
                    for run in now:
                        run()
        return 0

    lax.fori_loop(0, len(UNITS), unit, 0)


    for s in range(READY // SW, SUB):
        complete(s)
    for s in range(SUB):
        span = ys.at[s, pl.ds(0, 7)]
        remote(span, span, a0s.at[s], a0r.at[s], me).wait_send()
        remote(span, span, b0s.at[s], a0r.at[s], me).wait_send()

        @pl.when(odd != s % 2)
        def _():
            b0(s, 0, b0t.at[s]).wait_send()

        span = a_ref.at[pl.ds(0, 15), pl.ds(0, SW)]
        remote(span, span, a1s.at[s], a1f.at[s], me).wait_send()
    for f in range(2):
        span = b_ref.at[pl.ds(0, 7), f]
        remote(span, span, b1s.at[f], b1f.at[f], me).wait_send()


TURN, NEAR, FAR, PASS, PACE = 6, 8, 10, 10, 6
UNITS = (21, 24, 31.1, 33, 34, 35)
TM = 256
READY = 1536


def exchange(xt, index):
    vm = pl.BlockSpec(memory_space=pltpu.VMEM)
    dma = pltpu.SemaphoreType.DMA
    return pl.pallas_call(
        exchange_kernel,
        out_shape=(
            jax.ShapeDtypeStruct((COLS, GA, 128), jnp.bfloat16),
            jax.ShapeDtypeStruct((2, COLS * 128, GB), jnp.bfloat16),
            jax.ShapeDtypeStruct((2, 2, READY, SW), jnp.float32),
        ),
        in_specs=[vm, vm, vm],
        out_specs=(vm, vm, vm),
        scratch_shapes=[
            pltpu.VMEM((ROWS, 2, COLS, 16, SW), jnp.bfloat16),
            pltpu.VMEM((SUB, ROWS, 16, SW), jnp.bfloat16),
            pltpu.VMEM((SUB, ROWS, 16, SW), jnp.bfloat16),
            pltpu.VMEM((GA, 128), jnp.bfloat16),
            dma((SUB,)), dma((SUB,)),
            dma((SUB,)), dma((SUB,)), dma((2,)),
            dma((SUB,)), dma((SUB, 2, 12)), dma((SUB,)),
            dma((2,)), dma((2, 4)), dma((2,)),
            dma((SUB,)),
        ],
        compiler_params=pltpu.CompilerParams(
            collective_id=0, has_side_effects=True, vmem_limit_bytes=24 << 20
        ),
        name="exchange",
    )(xt, index.reshape(ROWS * SUB, SW), jnp.asarray(dft_tables()[3]))


TAIL = 128


def response_kernel(a_ref, rhs, part_ref, o_ref, stage, sems):
    copies = []

    def out(src, q, f, rows):
        copy = pltpu.make_async_copy(src, o_ref.at[q, rows, pl.ds(f * SW, SW)], sems.at[len(copies)])
        copy.start()
        copies.append(copy)

    for q in range(2):
        for f in range(2):
            out(part_ref.at[q, f], q, f, pl.ds(0, READY))
    for t in range((GA - READY) // TAIL):
        rows = pl.ds(READY + t * TAIL, TAIL)
        lhs = jnp.concatenate([a_ref[j, rows, :] for j in range(COLS)], axis=1)
        for f in range(2):
            for q in range(2):
                stage[t, q, f] = jnp.dot(
                    lhs, rhs[f, :, q * SW : (q + 1) * SW], preferred_element_type=jnp.float32
                )
                out(stage.at[t, q, f], q, f, rows)
    for copy in copies:
        copy.wait()


def contract(a, rhs, part):
    vm = pl.BlockSpec(memory_space=pltpu.VMEM)
    tiles = (GA - READY) // TAIL
    return pl.pallas_call(
        response_kernel,
        out_shape=jax.ShapeDtypeStruct((2, GA, GB), jnp.float32),
        in_specs=[vm, vm, vm],
        out_specs=pl.BlockSpec(memory_space=pltpu.HBM),
        scratch_shapes=[
            pltpu.VMEM((tiles, 2, 2, TAIL, SW), jnp.float32),
            pltpu.SemaphoreType.DMA((4 + 4 * tiles,)),
        ],
        compiler_params=pltpu.CompilerParams(vmem_limit_bytes=24 << 20),
        name="contract",
    )(a, rhs, part)


def body(valence, conduction, valence_energy, conduction_energy, band_pairs, grid_index):
    xt = spectrum(valence, conduction, valence_energy, conduction_energy, band_pairs)
    return contract(*exchange(xt, grid_index))


def solution(mesh):
    return jax.shard_map(
        body,
        mesh=mesh,
        in_specs=(P(), P(), P(), P(), P(("row", "col"), None), P()),
        out_specs=P(None, "row", "col"),
        check_vma=False,
    )
```

```python
import math
import numpy as np
import jax
import jax.numpy as jnp
import ml_dtypes
from jax import lax
from jax.sharding import PartitionSpec as P
from jax.experimental import pallas as pl
from jax.experimental.pallas import tpu as pltpu

N1 = N2 = N3 = 32
KA, KB = 256, 128
NGV = 16384
NR = 32768
GW = 2048


def split_np(t):
    hi = t.astype(ml_dtypes.bfloat16)
    lo = (t - hi.astype(np.float64)).astype(ml_dtypes.bfloat16)
    return hi, lo


def dft_tables():
    a = np.arange(KA)
    r1, r2a = a // 8, a % 8
    ph = (np.outer(r1, r1) / 32.0 + np.outer(r2a, r2a) / 8.0) % 1.0
    c, s = np.cos(2 * np.pi * ph), np.sin(2 * np.pi * ph)
    ta = np.block([[c, s], [-s, c]])
    b = np.arange(KB)
    r2b, r3 = b // 32, b % 32
    ph = (np.outer(r2b, r2b) / 4.0 + np.outer(r3, r3) / 32.0) % 1.0
    c, s = np.cos(2 * np.pi * ph), np.sin(2 * np.pi * ph)
    tb = np.block([[c, s], [-s, c]])
    ph = np.outer(r2a, r2b) / 32.0
    tw = np.stack([np.cos(2 * np.pi * ph), np.sin(2 * np.pi * ph)]).astype(np.float32)
    ta_hi, ta_lo = split_np(ta)
    tb_hi, tb_lo = split_np(tb)
    fold = np.zeros((16, 128), ml_dtypes.bfloat16)
    for p in range(8):
        for ri in range(2):
            fold[ri * 8 + p, p * 16 + ri * 8 : p * 16 + ri * 8 + 8] = 1
    return np.stack([ta_hi, ta_lo]), np.stack([tb_hi, tb_lo]), tw, fold


def split(x):
    hi = x.astype(jnp.bfloat16)
    return hi, (x - hi.astype(jnp.float32)).astype(jnp.bfloat16)


def dot_f32(a, b, dims):
    return lax.dot_general(a, b, (dims, ((), ())), preferred_element_type=jnp.float32)


def spectrum_kernel(
    bands, v_hbm, c_hbm, valence, conduction, ta_hbm, tb_hbm, tw_hbm, xt,
    v_energy, c_energy, v_half, c_half, v_full, c_full, ta, tb, tw, sems,
):
    tables = [
        pltpu.make_async_copy(src, dst, sems.at[k])
        for k, (src, dst) in enumerate(
            ((valence, v_half), (ta_hbm, ta), (tb_hbm, tb), (tw_hbm, tw), (v_hbm, v_energy), (c_hbm, c_energy))
        )
    ]

    def strip(p):
        rows = pl.ds(pl.multiple_of(bands[1, p] // 8 * 8, 8), 8)
        return pltpu.make_async_copy(conduction.at[:, rows, :], c_half.at[p], sems.at[6 + p])

    tables[0].start()
    strip(0).start()
    strip(1).start()
    for copy in tables[1:]:
        copy.start()
    for p in range(2, 8):
        strip(p).start()

    tables[0].wait()

    def widen_v(a, _):
        lanes = pl.ds(pl.multiple_of(a * 128, 128), 128)
        rows = pl.ds(pl.multiple_of(a * 16, 16), 16)
        for q in range(2):
            v_full[q, rows, :] = v_half[q, :, lanes].astype(jnp.float32)
        return 0

    lax.fori_loop(0, KA, widen_v, 0, unroll=8)

    nn = ((1,), (0,))
    nt = ((1,), (1,))

    def widen_c(h):
        for e in range(2):
            strip(2 * h + e).wait()
        for a in range(KA):
            for e in range(2):
                for q in range(2):
                    c_full[h % 2, e, q, a * 8 : a * 8 + 8, :] = c_half[
                        2 * h + e, q, :, a * 128 : a * 128 + 128
                    ].astype(jnp.float32)

    widen_c(0)
    for copy in tables[1:]:
        copy.wait()
    for h in range(4):
        real, imag = [], []
        for e in range(2):
            p = 2 * h + e
            vr, vi = (v_full[q, pl.ds(bands[0, p], KA, stride=16), :] for q in range(2))
            cr, ci = (c_full[h % 2, e, q, pl.ds(bands[1, p] % 8, KA, stride=8), :] for q in range(2))
            real.append(vr * cr + vi * ci)
            imag.append(vr * ci - vi * cr)
        x = jnp.concatenate([jnp.concatenate(real, axis=1), jnp.concatenate(imag, axis=1)], axis=0)
        xh, xl = split(x)
        z = dot_f32(
            jnp.concatenate([ta[0], ta[0], ta[1]], axis=1), jnp.concatenate([xh, xl, xh], axis=0), nn
        )
        if h < 3:
            widen_c(h + 1)
        for e in range(2):
            p = 2 * h + e
            zr, zi = z[:KA, e * KB : (e + 1) * KB], z[KA:, e * KB : (e + 1) * KB]
            t = jnp.concatenate([zr * tw[0] + zi * tw[1], zi * tw[0] - zr * tw[1]], axis=1)
            th, tl = split(t)
            s = dot_f32(
                jnp.concatenate([tb[0], tb[0], tb[1]], axis=1), jnp.concatenate([th, tl, th], axis=1), nt
            )
            gap = jnp.full((1, KA), v_energy[bands[0, p]] - c_energy[bands[1, p]], jnp.float32)
            scale = jnp.sqrt(-2.0 / (math.sqrt(1024) * gap)) * (1.0 / math.sqrt(N1 * N2 * N3))
            xt[p] = (s * scale).astype(jnp.bfloat16)


def spectrum(valence, conduction, valence_energy, conduction_energy, band_pairs):
    ta, tb, tw, _ = dft_tables()
    anywhere = pl.BlockSpec(memory_space=pltpu.HBM)
    scalars = pl.BlockSpec(memory_space=pltpu.SMEM)
    bf, f32 = jnp.bfloat16, jnp.float32
    return pl.pallas_call(
        spectrum_kernel,
        out_shape=jax.ShapeDtypeStruct((8, 256, 256), bf),
        in_specs=[scalars] + [anywhere] * 7,
        out_specs=pl.BlockSpec(memory_space=pltpu.VMEM),
        scratch_shapes=[
            pltpu.SMEM(valence_energy.shape, f32),
            pltpu.SMEM(conduction_energy.shape, f32),
            pltpu.VMEM((2, 16, NR), bf),
            pltpu.VMEM((8, 2, 8, NR), bf),
            pltpu.VMEM((2, KA * 16, 128), f32),
            pltpu.VMEM((2, 2, 2, KA * 8, 128), f32),
            pltpu.VMEM(ta.shape, bf),
            pltpu.VMEM(tb.shape, bf),
            pltpu.VMEM(tw.shape, f32),
            pltpu.SemaphoreType.DMA((14,)),
        ],
        compiler_params=pltpu.CompilerParams(vmem_limit_bytes=48 << 20),
        name="spectrum",
    )(band_pairs.T,
      *(pltpu.with_memory_space_constraint(t, pltpu.HBM)
        for t in (valence_energy, conduction_energy, valence, conduction, jnp.asarray(ta), jnp.asarray(tb), jnp.asarray(tw))))


MESH = pl.DeviceIdType.MESH
ROWS, COLS = 8, 16
GA, GB = NGV // ROWS, NGV // COLS
SUB, SW = 4, 512
HALF, PART = SW // 2, SW // 4
SIDES = ((0, 1), (1, 3))
SLOTS = (0, 3, 1, 2)


def exchange_kernel(
    xt, index_ref, fold_ref, a_ref, rhs, part_ref, b_ref, ys, pa, at,
    a0s, a0r, b0s, b0t, b0r, a1s, a1r, a1f, b1s, b1r, b1f, own_t,
):
    row, col = lax.axis_index("row"), lax.axis_index("col")
    x, core = row // 2, row % 2
    ty, tz, tx = ([(v + d) % 4 for d in range(4)] for v in (col // 4, col % 4, x))
    cell = [[ty[u] * 4 + tz[d] for d in range(4)] for u in range(4)]
    line = [tx[d] * 2 + core for d in range(4)]
    other = [tx[d] * 2 + 1 - core for d in range(4)]
    to_row = [(row + d) % ROWS for d in range(ROWS)]
    to_pair = [(col // 2 + d) % 8 for d in range(8)]
    odd = col % 2
    me = (row, col)

    def remote(src, dst, send, recv, device):
        return pltpu.make_async_remote_copy(
            src_ref=src, dst_ref=dst, send_sem=send, recv_sem=recv,
            device_id=device, device_id_type=MESH,
        )

    barrier = pltpu.get_barrier_semaphore()
    for d in range(1, ROWS):
        pl.semaphore_signal(barrier, inc=1, device_id=(to_row[d], col), device_id_type=MESH)
    for d in range(1, COLS):
        pl.semaphore_signal(barrier, inc=1, device_id=(row, (col + d) % COLS), device_id_type=MESH)

    def place(s):
        return s % 2 * 2 + s // 2


    def select(s, m):
        k = jnp.concatenate([index_ref[pl.ds(pl.multiple_of(((4 * m + e) * SUB + place(s)) * SW, SW), SW)].reshape(1, SW) for e in range(4)], axis=1)
        ka = (k >> 10) * 8 + ((k >> 5) & 7)
        kb = ((k >> 8) & 3) * 32 + (k & 31)
        hot = jnp.where(lax.broadcasted_iota(jnp.int32, (KA, GW), 0) == ka, 1.0, 0.0).astype(jnp.bfloat16)
        kb_hi = jnp.broadcast_to(kb >> 3, (8, GW))
        low = lax.broadcasted_iota(jnp.int32, (8, GW), 0) == (kb & 7)
        parts = []
        for p in range(8):
            r = jnp.dot(xt[p], hot, preferred_element_type=jnp.float32)
            for q in range(2):
                acc = r[q * KB : q * KB + 8]
                for j in range(1, 16):
                    acc = jnp.where(kb_hi == j, r[q * KB + j * 8 : q * KB + j * 8 + 8], acc)
                parts.append(jnp.where(low, acc, 0.0))
        part = jnp.concatenate(parts, axis=0).astype(jnp.bfloat16)
        y = jnp.dot(fold_ref[...], part, preferred_element_type=jnp.float32).astype(jnp.bfloat16)
        for e in range(4):
            ys[s, 4 * m + e] = y[:, e * SW : (e + 1) * SW]


    def b0(s, d, sem):
        i = to_pair[d]
        return remote(ys.at[s, i], b_ref.at[row, s // 2, col], sem, b0r.at[s // 2], (row, 2 * i + s % 2))

    def hand_out(s):
        if s == 0:
            pl.semaphore_wait(barrier, ROWS + COLS - 2)
        for d in range(1, ROWS):
            i = to_row[d]
            remote(ys.at[s, i], pa.at[s, row], a0s.at[s], a0r.at[s], (i, col)).start()
        pltpu.make_async_copy(ys.at[s, row], pa.at[s, row], a0r.at[s]).start()
        for d in range(1, 8):
            b0(s, d, b0s.at[s]).start()

        @pl.when(odd == s % 2)
        def _():
            pltpu.make_async_copy(ys.at[s, to_pair[0]], b_ref.at[row, s // 2, col], b0r.at[s // 2]).start()

        @pl.when(odd != s % 2)
        def _():
            b0(s, 0, b0t.at[s]).start()


    def along(h, first, d):
        return (row, cell[d][0] if (h == 0) == first else cell[0][d])

    def spot(h, u, d):
        return cell[u][d] if h == 0 else cell[d][u]

    def rows(s, h, part=None):
        if part is None:
            return pl.ds(place(s) * SW + h * HALF, HALF)
        return pl.ds(place(s) * SW + h * HALF + part * PART, PART)

    def a1(s, h, k, j, device, part=None, src=None):
        dst = a_ref.at[j, rows(s, h, part)]
        recv = a1f.at[s] if k is None else a1r.at[s, h, k]
        return remote(dst if src is None else src, dst, a1s.at[s], recv, device)

    def second(s, h, slot):
        u = SLOTS[slot]
        src = at.at[rows(s, h)] if u == 0 else None
        for n, d in SIDES:
            a1(s, h, 4 + slot * 2 + n, spot(h, u, 0), along(h, False, d), src=src).start()

    def keep_t(s):
        span = pl.ds(place(s) * SW, SW)
        return pltpu.make_async_copy(at.at[span], a_ref.at[col, span], own_t.at[s])

    def turn(s):
        remote(pa.at[s], pa.at[s], a0s.at[s], a0r.at[s], me).wait_recv()
        for n in range(SW // 128):
            block = pa[s, :, :, n * 128 : (n + 1) * 128].reshape(128, 128)
            start = place(s) * SW + n * 128
            at[start : start + 128, :] = block.astype(jnp.float32).T.astype(jnp.bfloat16)
        for h in range(2):
            for n, d in SIDES:
                a1(s, h, n, col, along(h, True, d), src=at.at[rows(s, h)]).start()
        for h in range(2):
            second(s, h, 0)
        keep_t(s).start()

    def near(s):
        for n, d in SIDES:
            for h in range(2):
                j = spot(h, 4 - d, 0)
                a1(s, h, n, j, me).wait_recv()
                a1(s, h, 2 + n, j, along(h, True, d), part=n).start()
                second(s, h, 1 + n)

    def far(s):
        for h in range(2):
            for n in range(2):
                a1(s, h, 2 + n, spot(h, 2, 0), me, part=n).wait_recv()
            second(s, h, 3)

    def pass_on(s, slot):
        u = SLOTS[slot]
        for n, d in SIDES:
            for h in range(2):
                j = spot(h, u, 4 - d)
                a1(s, h, 4 + slot * 2 + n, j, me).wait_recv()
                a1(s, h, None, j, along(h, False, d), part=n).start()


    def b1(f, k, i, device, part=None):
        ref = b_ref.at[i, f] if part is None else b_ref.at[i, f, pl.ds(part * 8, 8)]
        return remote(ref, ref, b1s.at[f], b1f.at[f] if k is None else b1r.at[f, k], device)

    def sides(f):
        ref = b_ref.at[row, f]
        remote(ref, ref, b1s.at[f], b0r.at[f], me).wait_recv()
        for n, d in SIDES:
            b1(f, n, row, (line[d], col)).start()
        b1(f, None, row, (other[0], col)).start()

    def sides_near(f):
        for n, d in SIDES:
            i = line[4 - d]
            b1(f, n, i, me).wait_recv()
            b1(f, 2 + n, i, (line[d], col), part=n).start()
            b1(f, None, i, (other[0], col)).start()

    def sides_far(f):
        for n in range(2):
            b1(f, 2 + n, line[2], me, part=n).wait_recv()
            b1(f, None, line[2], (other[0], col), part=n).start()


    events = []
    for s in range(SUB):
        events.append((4 * s + 3.9, lambda s=s: hand_out(s)))
        events.append((4 * s + TURN, lambda s=s: turn(s)))
        events.append((4 * s + NEAR, lambda s=s: near(s)))
        events.append((4 * s + FAR, lambda s=s: far(s)))
        for slot in range(4):
            events.append((PASS + PACE * s + 1.5 * slot, lambda s=s, slot=slot: pass_on(s, slot)))
        for delay, run in ((7.1, sides), (11.6, sides_near), (15.4, sides_far)):
            def guarded(s=s, run=run):
                @pl.when(odd == s % 2)
                def _():
                    run(s // 2)

            events.append((4 * s + delay, guarded))
    events.sort(key=lambda e: e[0])

    def step(n, _):
        select(n // 2, n % 2)
        for k in range(8):
            now = [run for time, run in events if 2 * k + 1.5 <= time < 2 * k + 3.5]
            if now:
                @pl.when(n == k)
                def _(now=now):
                    for run in now:
                        run()
        return 0

    lax.fori_loop(0, 8, step, 0)
    for time, run in events:
        if 17.5 <= time < UNITS[0]:
            run()


    def build(f):
        span = b_ref.at[pl.ds(0, 4), f]
        remote(span, span, b1s.at[f], b1f.at[f], me).wait_recv()

        def cross(n, _):
            i, j = n // COLS, n % COLS
            block = b_ref[i, f, j].astype(jnp.float32)
            span = pl.ds(pl.multiple_of(j * 128 + i * 16, 16), 16)
            rhs[f, span, :SW] = (-block).astype(jnp.bfloat16)
            rhs[f, span, SW:] = jnp.concatenate([-block[8:], block[:8]], axis=0).astype(jnp.bfloat16)
            return 0

        lax.fori_loop(0, ROWS * COLS, cross, 0, unroll=4)

    def complete(s):
        whole = a_ref.at[0]
        remote(whole, whole, a1s.at[s], a1f.at[s], me).wait_recv()
        keep_t(s).wait()

    ready = {0: [lambda: complete(0), lambda: build(0)], 1: [lambda: complete(1)], 2: [lambda: build(1)],
             4: [lambda: complete(2)]}

    def unit(t, _):
        for k, runs in ready.items():
            @pl.when(t == k)
            def _(runs=runs):
                for run in runs:
                    run()

        late = t // 4
        f = (1 - late) * (t // 2) + late * (t % 2)
        block = (1 - late) * (t % 2) * 2 + late
        for e in range(SW // TM):
            span = pl.ds(pl.multiple_of(block * SW + e * TM, TM), TM)
            lhs = jnp.concatenate([a_ref[j, span, :] for j in range(COLS)], axis=1)
            for q in range(2):
                part_ref[q, f, span, :] = jnp.dot(
                    lhs, rhs[f, :, q * SW : (q + 1) * SW], preferred_element_type=jnp.float32
                )
        for k in range(len(UNITS)):
            upper = UNITS[k + 1] if k + 1 < len(UNITS) else 1e9
            now = [run for time, run in events if UNITS[k] <= time < upper]
            if now:
                @pl.when(t == k)
                def _(now=now):
                    for run in now:
                        run()
        return 0

    lax.fori_loop(0, len(UNITS), unit, 0)


    for s in range(READY // SW, SUB):
        complete(s)
    for s in range(SUB):
        span = ys.at[s, pl.ds(0, 7)]
        remote(span, span, a0s.at[s], a0r.at[s], me).wait_send()
        remote(span, span, b0s.at[s], a0r.at[s], me).wait_send()

        @pl.when(odd != s % 2)
        def _():
            b0(s, 0, b0t.at[s]).wait_send()

        span = a_ref.at[pl.ds(0, 15), pl.ds(0, SW)]
        remote(span, span, a1s.at[s], a1f.at[s], me).wait_send()
    for f in range(2):
        span = b_ref.at[pl.ds(0, 7), f]
        remote(span, span, b1s.at[f], b1f.at[f], me).wait_send()


TURN, NEAR, FAR, PASS, PACE = 6, 8, 10, 10, 6
UNITS = (21, 24, 31.1, 33, 34, 35)
TM = 256
READY = 1536


def exchange(xt, index):
    vm = pl.BlockSpec(memory_space=pltpu.VMEM)
    dma = pltpu.SemaphoreType.DMA
    return pl.pallas_call(
        exchange_kernel,
        out_shape=(
            jax.ShapeDtypeStruct((COLS, GA, 128), jnp.bfloat16),
            jax.ShapeDtypeStruct((2, COLS * 128, GB), jnp.bfloat16),
            jax.ShapeDtypeStruct((2, 2, READY, SW), jnp.float32),
        ),
        in_specs=[vm, vm, vm],
        out_specs=(vm, vm, vm),
        scratch_shapes=[
            pltpu.VMEM((ROWS, 2, COLS, 16, SW), jnp.bfloat16),
            pltpu.VMEM((SUB, ROWS, 16, SW), jnp.bfloat16),
            pltpu.VMEM((SUB, ROWS, 16, SW), jnp.bfloat16),
            pltpu.VMEM((GA, 128), jnp.bfloat16),
            dma((SUB,)), dma((SUB,)),
            dma((SUB,)), dma((SUB,)), dma((2,)),
            dma((SUB,)), dma((SUB, 2, 12)), dma((SUB,)),
            dma((2,)), dma((2, 4)), dma((2,)),
            dma((SUB,)),
        ],
        compiler_params=pltpu.CompilerParams(
            collective_id=0, has_side_effects=True, vmem_limit_bytes=24 << 20
        ),
        name="exchange",
    )(xt, index, jnp.asarray(dft_tables()[3]))


TAIL = 128


def response_kernel(a_ref, rhs, part_ref, o_ref, stage, sems):
    copies = []

    def out(src, q, f, rows):
        copy = pltpu.make_async_copy(src, o_ref.at[q, rows, pl.ds(f * SW, SW)], sems.at[len(copies)])
        copy.start()
        copies.append(copy)

    for q in range(2):
        for f in range(2):
            out(part_ref.at[q, f], q, f, pl.ds(0, READY))
    for t in range((GA - READY) // TAIL):
        rows = pl.ds(READY + t * TAIL, TAIL)
        lhs = jnp.concatenate([a_ref[j, rows, :] for j in range(COLS)], axis=1)
        for f in range(2):
            for q in range(2):
                stage[t, q, f] = jnp.dot(
                    lhs, rhs[f, :, q * SW : (q + 1) * SW], preferred_element_type=jnp.float32
                )
                out(stage.at[t, q, f], q, f, rows)
    for copy in copies:
        copy.wait()


def contract(a, rhs, part):
    vm = pl.BlockSpec(memory_space=pltpu.VMEM)
    tiles = (GA - READY) // TAIL
    return pl.pallas_call(
        response_kernel,
        out_shape=jax.ShapeDtypeStruct((2, GA, GB), jnp.float32),
        in_specs=[vm, vm, vm],
        out_specs=pl.BlockSpec(memory_space=pltpu.HBM),
        scratch_shapes=[
            pltpu.VMEM((tiles, 2, 2, TAIL, SW), jnp.float32),
            pltpu.SemaphoreType.DMA((4 + 4 * tiles,)),
        ],
        compiler_params=pltpu.CompilerParams(vmem_limit_bytes=24 << 20),
        name="contract",
    )(a, rhs, part)


def body(valence, conduction, valence_energy, conduction_energy, band_pairs, grid_index):
    xt = spectrum(valence, conduction, valence_energy, conduction_energy, band_pairs)
    return contract(*exchange(xt, grid_index))


def solution(mesh):
    return jax.shard_map(
        body,
        mesh=mesh,
        in_specs=(P(), P(), P(), P(), P(("row", "col"), None), P()),
        out_specs=P(None, "row", "col"),
        check_vma=False,
    )
```
